256 devices in a mesh: seq: 32 (over x_hi, z, core), tensor: 8 (over x_lo, y).
Axes of the slice: x: 4 (x_hi: 2, x_lo: 2; x = x_hi * 2 + x_lo), y: 4, z: 8, core: 2. Of those that a mesh axis runs over, the one named last changes fastest.
Arguments:
- hidden: bfloat16 [8192, 2304], P('seq', 'tensor'), may hold values from -6 to 6
- attn_gain: float32 [2304], replicated, may hold values from 0.1 to 1.9
- query_weight: bfloat16 [2304, 2048], P(None, 'tensor'), may hold values from -1 to 1
- kv_weight: bfloat16 [2304, 2048], P(None, 'tensor'), may hold values from -1 to 1
- out_weight: bfloat16 [2048, 2304], P('tensor'), may hold values from -0.125 to 0.125
- post_gain: float32 [2304], replicated, may hold values from 0.1 to 1.9
- ff_gain: float32 [2304], replicated, may hold values from 0.1 to 1.9
- ff_post_gain: float32 [2304], replicated, may hold values from 0.1 to 1.9
- gate_weight: bfloat16 [2304, 9216], P('seq', 'tensor'), may hold values from -0.125 to 0.125
- up_weight: bfloat16 [2304, 9216], P('seq', 'tensor'), may hold values from -0.125 to 0.125
- down_weight_t: bfloat16 [2304, 9216], P('seq', 'tensor'), may hold values from -0.0625 to 0.0625
- next_gain: float32 [2304], replicated, may hold values from 0.1 to 1.9
- next_query_weight: bfloat16 [2304, 2048], P(None, 'tensor'), may hold values from -0.125 to 0.125
- next_kv_weight: bfloat16 [2304, 2048], P(None, 'tensor'), may hold values from -0.125 to 0.125
- lengths: int32 [4], replicated, may hold values from 256 to 3840, as said below
- pair_owner: int32 [32], replicated, may hold values from 0 to 31, each once
- page_table: int32 [64], replicated, may hold values from 0 to 63, each once
Outputs:
- hidden_out: bfloat16 [8192, 2304], P('seq', 'tensor')
- next_query: bfloat16 [8192, 2048], P('seq', 'tensor')
- next_kv: bfloat16 [8192, 2048], P('seq', 'tensor')
- kv_pages: bfloat16 [64, 128, 2048], P('seq', None, 'tensor')
The draws below stay inside these ranges and needn't reach their ends.
Inputs may be any that keep to these rules, and one draw needn't show every extreme that they name: Four positive lengths summing to 8192; the first is the longest and the fourth the shortest. `pair_owner`: each mirrored pair b, the blocks b and 63 - b, is held by exactly one index of seq. `page_table`: every page takes exactly one block.
All inputs are finite; a program needn't handle non-finite values.
Results may differ from the reference program's by a relative error of at most 0.018.
Values may be sent and summed in bfloat16 or wider, within the bound.
A program may use at most 128 MiB of HBM per device.

```python
import math
import jax
import jax.numpy as jnp
from jax import lax

D = 2304
FF = 9216
HD = 256
QH = 8
KVH = 4
TOK_DEV = 256
BLK = 128
TOKENS = 8192
BLOCKS = 64
N_SEQ = 32


def draw_lengths(key, part):
    third_len = jax.random.randint(key, (), TOKENS // 32 + 1, TOKENS // 4 + 1)
    first_len = 15 * TOKENS // 32
    fourth_len = TOKENS // 32
    second_len = TOKENS - first_len - fourth_len - third_len
    return jnp.stack([jnp.int32(first_len) + 0 * third_len, second_len, third_len, jnp.int32(fourth_len) + 0 * third_len]).astype(jnp.int32)


def drawn_projection(key, column_count, column_mask, salt):
    direction = jnp.clip(jax.random.normal(jax.random.fold_in(key, 101), (D,), jnp.float32), -6.0, 6.0)
    base = jnp.clip(jax.random.normal(jax.random.fold_in(key, salt), (D, column_count), jnp.float32), -6.0, 6.0)
    strength = 5.0
    amplitude = math.sqrt(strength * math.sqrt(HD) / 8.0)
    pattern = column_mask.astype(jnp.float32)
    combined = (base + amplitude * direction[:, None] * pattern[None, :]) / math.sqrt(D)
    return jnp.clip(combined, -1.0, 1.0)


def draw_query_weight(key, part):
    column = jnp.arange(QH * HD, dtype=jnp.int32)
    within = column % HD
    column_mask = within % (HD // 2) >= HD // 2 - 4
    return drawn_projection(key, QH * HD, column_mask, 1).astype(jnp.bfloat16)


def draw_kv_weight(key, part):
    column = jnp.arange(2 * KVH * HD, dtype=jnp.int32)
    within = column % HD
    column_mask = (within % (HD // 2) >= HD // 2 - 4) & (column % (2 * HD) < HD)
    return drawn_projection(key, 2 * KVH * HD, column_mask, 2).astype(jnp.bfloat16)


def steps_of(stream_key, dims, pieces, smallest, high):
    gain, own = 1.0, jax.random.fold_in(stream_key, 6)
    for axis_at, shards_of in pieces:
        draws = jnp.exp(jax.random.uniform(jax.random.fold_in(own, axis_at), (shards_of,), jnp.float32, smallest / len(pieces), high / len(pieces)))
        gain = gain * jnp.repeat(draws, dims[axis_at] // shards_of).reshape([-1 if axis == axis_at else 1 for axis in range(len(dims))])
    return gain


def gaussian(stream_key, extent, spread, reach, cuts=(), held_as=jnp.bfloat16):
    gain = steps_of(stream_key, extent, cuts, -0.22, 0.18) if cuts else 1.0
    drawn = jax.random.normal(stream_key, extent, jnp.float32) * spread * gain
    return jnp.minimum(jnp.maximum(drawn, -reach), reach).astype(held_as)


def setup_inputs(seed: int = 0) -> dict:
    key_list = jax.random.split(jax.random.key(seed), 18)
    hidden = gaussian(key_list[0], (TOKENS, D), 1.0, 6.0, ((0, 32), (1, 8)))
    attn_gain = jnp.clip(1.0 + 0.18 * jax.random.normal(key_list[1], (D,), jnp.float32), 0.1, 1.9)
    query_weight = draw_query_weight(jax.random.fold_in(key_list[17], 71), 0)
    kv_weight = draw_kv_weight(jax.random.fold_in(key_list[17], 71), 0)
    out_weight = gaussian(key_list[4], (QH * HD, D), (QH * HD) ** -0.5, 0.125, ((0, 8),))
    post_gain = jnp.clip(1.0 + 0.18 * jax.random.normal(key_list[5], (D,), jnp.float32), 0.1, 1.9)
    ff_gain = jnp.clip(1.0 + 0.18 * jax.random.normal(key_list[6], (D,), jnp.float32), 0.1, 1.9)
    ff_post_gain = jnp.clip(1.0 + 0.18 * jax.random.normal(key_list[7], (D,), jnp.float32), 0.1, 1.9)
    gate_weight = gaussian(key_list[8], (D, FF), D ** -0.5, 0.125, ((0, 32), (1, 8)))
    up_weight = gaussian(key_list[9], (D, FF), D ** -0.5, 0.125, ((0, 32), (1, 8)))
    down_weight_t = gaussian(key_list[10], (D, FF), FF ** -0.5, 0.0625, ((0, 32), (1, 8)))
    next_gain = jnp.clip(1.0 + 0.18 * jax.random.normal(key_list[11], (D,), jnp.float32), 0.1, 1.9)
    next_query_weight = gaussian(key_list[12], (D, QH * HD), D ** -0.5, 0.125, ((1, 8),))
    next_kv_weight = gaussian(key_list[13], (D, 2 * KVH * HD), D ** -0.5, 0.125, ((1, 8),))
    lengths = draw_lengths(jax.random.fold_in(key_list[17], 71), 0)
    pair_owner = jax.random.permutation(key_list[15], N_SEQ).astype(jnp.int32)
    page_table = jax.random.permutation(key_list[16], BLOCKS).astype(jnp.int32)
    return dict(hidden=hidden, attn_gain=attn_gain, query_weight=query_weight, kv_weight=kv_weight, out_weight=out_weight, post_gain=post_gain, ff_gain=ff_gain, ff_post_gain=ff_post_gain, gate_weight=gate_weight, up_weight=up_weight, down_weight_t=down_weight_t, next_gain=next_gain, next_query_weight=next_query_weight, next_kv_weight=next_kv_weight, lengths=lengths, pair_owner=pair_owner, page_table=page_table)


EPS = 1e-06
SOFT_CAP = 50.0

def row_norm(values, gain_vec):
    values = values.astype(jnp.float32)
    scale_vec = lax.rsqrt(lax.optimization_barrier(jnp.mean(values * values, axis=-1, keepdims=True)) + EPS)
    return values * scale_vec * gain_vec

def rotate(values, positions):
    half_dim = values.shape[-1] // 2
    freq_vec = 10000.0 ** (-jnp.arange(half_dim, dtype=jnp.float32) / half_dim)
    angles = positions.astype(jnp.float32)[:, None, None] * freq_vec[None, None, :]
    cosine_val = jnp.cos(angles)
    sine_val = jnp.sin(angles)
    leading = values[..., :half_dim]
    trailing = values[..., half_dim:]
    return jnp.concatenate([leading * cosine_val - trailing * sine_val, trailing * cosine_val + leading * sine_val], axis=-1)

def tenant_of(stream_index, lengths):
    tenant_ends = jnp.cumsum(lengths).astype(jnp.int32)
    tenant_starts = (tenant_ends - lengths).astype(jnp.int32)
    tenant = lax.optimization_barrier(jnp.sum((stream_index[:, None] >= tenant_ends[None, :3]).astype(jnp.int32), axis=1)).astype(jnp.int32)
    selector = tenant[:, None] == jnp.arange(4, dtype=jnp.int32)[None, :]
    offset = lax.optimization_barrier(jnp.sum(jnp.where(selector, tenant_starts[None, :], 0), axis=1)).astype(jnp.int32)
    return (tenant, (stream_index - offset).astype(jnp.int32))

def stream_tags(pair_owner, rows_half):
    block_count = 2 * pair_owner.shape[0]
    local_range = jnp.arange(rows_half, dtype=jnp.int32)[None, :]
    leading = pair_owner[:, None] * rows_half + local_range
    trailing = (block_count - 1 - pair_owner)[:, None] * rows_half + local_range
    return jnp.concatenate([leading, trailing], axis=1).reshape(-1).astype(jnp.int32)

def reference(hidden, attn_gain, query_weight, kv_weight, out_weight, post_gain, ff_gain, ff_post_gain, gate_weight, up_weight, down_weight_t, next_gain, next_query_weight, next_kv_weight, lengths, pair_owner, page_table):
    rows_half = TOK_DEV // 2
    tags = stream_tags(pair_owner, rows_half)
    tenant, position = tenant_of(tags, lengths)
    attn_input = row_norm(hidden, attn_gain).astype(jnp.bfloat16)
    query_proj = jnp.dot(attn_input, query_weight, preferred_element_type=jnp.float32).reshape(TOKENS, QH, HD)
    queries = rotate(query_proj, position).astype(jnp.bfloat16)
    kv_proj = jnp.dot(attn_input, kv_weight, preferred_element_type=jnp.float32).reshape(TOKENS, KVH, 2, HD)
    key_all = rotate(kv_proj[:, :, 0], position).astype(jnp.bfloat16)
    value_all = kv_proj[:, :, 1].astype(jnp.bfloat16)
    q_block = min(TOKENS, 1024)
    block_count = TOKENS // q_block
    query_scale = HD ** (-0.5)

    def attend(flat_index):
        head_index = flat_index // block_count
        row_start = flat_index % block_count * q_block
        query_rows = lax.dynamic_slice_in_dim(queries, row_start, q_block, 0)
        query_head = lax.dynamic_index_in_dim(query_rows, head_index, 1, keepdims=False)
        key_head = lax.dynamic_index_in_dim(key_all, head_index // 2, 1, keepdims=False)
        value_head = lax.dynamic_index_in_dim(value_all, head_index // 2, 1, keepdims=False)
        query_tags = lax.dynamic_slice_in_dim(tags, row_start, q_block, 0)
        query_tenant = lax.dynamic_slice_in_dim(tenant, row_start, q_block, 0)
        raw_scores = jnp.dot(query_head, key_head.T, preferred_element_type=jnp.float32) * query_scale
        capped = SOFT_CAP * jnp.tanh(raw_scores / SOFT_CAP)
        allowed = (query_tenant[:, None] == tenant[None, :]) & (tags[None, :] <= query_tags[:, None])
        weights = jnp.where(allowed, jnp.exp(capped), 0.0).astype(jnp.bfloat16)
        denominator = lax.optimization_barrier(jnp.sum(weights.astype(jnp.float32), axis=1))
        numerator = jnp.dot(weights, value_head, preferred_element_type=jnp.float32)
        return (numerator / denominator[:, None]).astype(jnp.bfloat16)
    blocks_out = lax.map(attend, jnp.arange(QH * block_count, dtype=jnp.int32))
    attended = blocks_out.reshape(QH, TOKENS, HD).transpose(1, 0, 2).reshape(TOKENS, QH * HD)
    attn_sum = jnp.dot(attended, out_weight, preferred_element_type=jnp.float32)
    middle = (hidden.astype(jnp.float32) + row_norm(attn_sum, post_gain)).astype(jnp.bfloat16)
    ff_input = row_norm(middle, ff_gain).astype(jnp.bfloat16)
    gate_val = jnp.dot(ff_input, gate_weight, preferred_element_type=jnp.float32)
    up_val = jnp.dot(ff_input, up_weight, preferred_element_type=jnp.float32)
    inner = (jax.nn.gelu(gate_val, approximate=True) * up_val).astype(jnp.bfloat16)
    ff_sum = jnp.dot(inner, down_weight_t.T, preferred_element_type=jnp.float32)
    hidden_out = (middle.astype(jnp.float32) + row_norm(ff_sum, ff_post_gain)).astype(jnp.bfloat16)
    next_input = row_norm(hidden_out, next_gain).astype(jnp.bfloat16)
    next_q_proj = jnp.dot(next_input, next_query_weight, preferred_element_type=jnp.float32).reshape(TOKENS, QH, HD)
    next_query = rotate(next_q_proj, position).reshape(TOKENS, QH * HD).astype(jnp.bfloat16)
    next_kv_proj = jnp.dot(next_input, next_kv_weight, preferred_element_type=jnp.float32).reshape(TOKENS, KVH, 2, HD)
    next_keys = rotate(next_kv_proj[:, :, 0], position)
    next_kv = jnp.stack([next_keys, next_kv_proj[:, :, 1]], axis=2).reshape(TOKENS, KVH * 2 * HD).astype(jnp.bfloat16)
    kv_rows = jnp.stack([key_all, value_all], axis=2).reshape(TOKENS, KVH * 2 * HD)
    stream_rows = jnp.zeros((TOKENS, KVH * 2 * HD), jnp.bfloat16).at[tags].set(kv_rows)
    kv_pages = jnp.zeros((BLOCKS, BLK, KVH * 2 * HD), jnp.bfloat16).at[page_table].set(stream_rows.reshape(BLOCKS, BLK, KVH * 2 * HD))
    return (hidden_out, next_query, next_kv, kv_pages)
```

```python
import functools

import jax
import jax.numpy as jnp
from jax import lax
from jax.experimental import pallas as pl
from jax.experimental.pallas import tpu as pltpu
from jax.sharding import PartitionSpec as P

EPS = 1e-06
SOFT_CAP = 50.0
MESH = pl.DeviceIdType.MESH
VM = pl.BlockSpec(memory_space=pltpu.VMEM)
AN = pl.BlockSpec(memory_space=pl.ANY)
FFP = 640
FFO = 512
bf16 = jnp.bfloat16
f32 = jnp.float32


class Place:
    def __init__(self):
        self.s = lax.axis_index("seq")
        self.t = lax.axis_index("tensor")
        self.x = self.s // 16
        self.z = (self.s // 2) % 8
        self.c = self.s % 2
        self.yb = self.t % 2

    def seq(self, x, z, c):
        return x * 16 + z * 2 + c

    def dev(self, s, t):
        return {"seq": s, "tensor": t}

    def zp(self):
        return self.dev(self.seq(self.x, (self.z + 1) % 8, self.c), self.t)

    def zm(self):
        return self.dev(self.seq(self.x, (self.z + 7) % 8, self.c), self.t)

    def sib(self):
        return self.dev(self.seq(self.x, self.z, 1 - self.c), self.t)

    def xpart(self):
        return self.dev(self.seq(1 - self.x, self.z, self.c), self.t)

    def quad(self, o):
        dx, dy = o // 2, o % 2
        x = (self.x + dx) % 2
        yb = (self.yb + dy) % 2
        return x, yb, self.dev(self.seq(x, self.z, self.c), self.t - self.yb + yb)

    def tens(self, o):
        t = (self.t + o) % 8
        return t, self.dev(self.s, t)

    def plane(self, o):
        j = (self.x * 8 + self.t + o) % 16
        x, t = j // 8, j % 8
        return j, self.dev(self.seq(x, self.z, self.c), t)


class Copies:
    def __init__(self, send, recv):
        self.send, self.recv, self.n, self.live = send, recv, 0, []

    def make(self, src, dst, dev):
        i = self.n
        self.n += 1
        return pltpu.make_async_remote_copy(
            src_ref=src, dst_ref=dst, send_sem=self.send.at[i], recv_sem=self.recv.at[i],
            device_id=dev, device_id_type=MESH,
        )

    def go(self, src, dst, dev):
        cp = self.make(src, dst, dev)
        cp.start()
        self.live.append(cp)
        return cp

    def drain_sends(self):
        for cp in self.live:
            cp.wait_send()


def barrier(peers):
    sem = pltpu.get_barrier_semaphore()
    for dev in peers:
        pl.semaphore_signal(sem, inc=1, device_id=dev, device_id_type=MESH)
    pl.semaphore_wait(sem, len(peers))


def weight_round(p, cps, ws, d):
    got = []
    right = ((p.z + 9 - d) % 8) * 2 + p.c
    left = ((p.z + 7 + d) % 8) * 2 + p.c
    for w in ws:
        if d < 4:
            got.append((cps.go(w.at[:, right], w.at[:, right], p.zp()), w))
            got.append((cps.go(w.at[:, left], w.at[:, left], p.zm()), w))
        else:
            got.append((cps.go(w.at[0, right], w.at[0, right], p.zp()), w))
            got.append((cps.go(w.at[1, left], w.at[1, left], p.zm()), w))
    return got


def weight_finish(p, cps, ws, got, d):
    right = ((p.z + 8 - d) % 8) * 2 + p.c
    left = ((p.z + d) % 8) * 2 + p.c
    out = []
    for i, (cp, w) in enumerate(got):
        cp.wait_recv()
        if d < 4:
            slot = right if i % 2 == 0 else left
            out.append(cps.go(w.at[:, slot], w.at[:, slot], p.sib()))
        elif i % 2 == 1:
            out.append(cps.go(w.at[:, right], w.at[:, right], p.sib()))
    return out


def gather_hidden(ht, gate, up, down, xt, wg, wu, wd, send, recv, loc):
    p = Place()
    peers = [p.tens(o)[1] for o in range(1, 8)] + [p.xpart(), p.zp(), p.zm(), p.sib()]
    barrier(peers)
    cps = Copies(send, recv)
    ws = (wg, wu, wd)
    slot = p.z * 2 + p.c
    mine = pl.ds(pl.multiple_of(p.x * FFO, 128), FFP)
    other = pl.ds(pl.multiple_of((1 - p.x) * FFO, 128), FFP)
    swaps = [cps.go(a.at[:, other], w.at[p.x, slot], p.xpart()) for a, w in zip((gate, up, down), ws)]
    locs = [pltpu.make_async_copy(a.at[:, mine], w.at[p.x, slot], loc.at[i])
            for i, (a, w) in enumerate(zip((gate, up, down), ws))]
    rows = pl.ds(pl.multiple_of(p.t * 288, 32), 288)
    locs.append(pltpu.make_async_copy(ht, xt.at[rows], loc.at[3]))
    for cp in locs:
        cp.start()
    hid = [cps.go(ht, xt.at[rows], p.tens(o)[1]) for o in range(1, 8)]
    for cp in locs:
        cp.wait()
    for cp in swaps:
        cp.wait_recv()
    got = weight_round(p, cps, ws, 1)
    sib = [cps.go(w.at[:, slot], w.at[:, slot], p.sib()) for w in ws]
    sib += weight_finish(p, cps, ws, got, 1)
    for cp in hid + sib:
        cp.wait_recv()
    cps.drain_sends()


def exchange_kv(stay, go, q, kv, qa, send, recv, loc):
    p = Place()
    quads = [p.quad(o) for o in range(1, 4)]
    barrier([d for _, _, d in quads] + [p.zp(), p.zm(), p.sib()])
    cps = Copies(send, recv)
    slot = p.z * 2 + p.c
    locs = [pltpu.make_async_copy(stay, kv.at[p.yb, slot], loc.at[0]),
            pltpu.make_async_copy(q, qa.at[p.x * 2 + p.yb], loc.at[1])]
    for cp in locs:
        cp.start()
    pair = cps.go(go, kv.at[p.yb, slot], quads[0][2])
    qs = [cps.go(q, qa.at[p.x * 2 + p.yb], d) for _, _, d in quads]
    for cp in locs:
        cp.wait()
    pair.wait_recv()
    got = weight_round(p, cps, (kv,), 1)
    sib = [cps.go(kv.at[:, slot], kv.at[:, slot], p.sib())]
    for d in range(1, 5):
        for cp, _ in got:
            cp.wait_recv()
        nxt = weight_round(p, cps, (kv,), d + 1) if d < 4 else []
        right = ((p.z + 8 - d) % 8) * 2 + p.c
        left = ((p.z + d) % 8) * 2 + p.c
        sib.append(cps.go(kv.at[:, right], kv.at[:, right], p.sib()))
        if d < 4:
            sib.append(cps.go(kv.at[:, left], kv.at[:, left], p.sib()))
        got = nxt
    for cp in qs + sib:
        cp.wait_recv()
    cps.drain_sends()


def weight_tail(p, cps, ws, d):
    got = weight_round(p, cps, ws, d)
    return weight_finish(p, cps, ws, got, d)


def exchange_partials(part, wg0, wu0, wd0, rx, wg, wu, wd, send, recv):
    p = Place()
    quads = [p.quad(o) for o in range(1, 4)]
    barrier([d for _, _, d in quads] + [p.zp(), p.zm(), p.sib()])
    cps = Copies(send, recv)
    ex = [cps.go(part.at[x * 2 + yb], rx.at[o], d) for o, (x, yb, d) in enumerate(quads)]
    sib = weight_tail(p, cps, (wg, wu, wd), 2)
    for cp in ex + sib:
        cp.wait_recv()
    cps.drain_sends()


def scatter_tensor(o_ref, wg0, wu0, wd0, rx, wg, wu, wd, send, recv):
    p = Place()
    tens = [p.tens(o) for o in range(1, 8)]
    barrier([d for _, d in tens] + [p.zp(), p.zm(), p.sib()])
    cps = Copies(send, recv)
    ex = [cps.go(o_ref.at[t], rx.at[i], d) for i, (t, d) in enumerate(tens)]
    sib = weight_tail(p, cps, (wg, wu, wd), 3)
    for cp in ex + sib:
        cp.wait_recv()
    cps.drain_sends()


def gather_plane(f_ref, wg0, wu0, wd0, xa, wg, wu, wd, send, recv, loc):
    p = Place()
    plane = [p.plane(o) for o in range(1, 16)]
    barrier([d for _, d in plane] + [p.zp(), p.zm(), p.sib()])
    cps = Copies(send, recv)
    own = p.x * 8 + p.t
    lc = pltpu.make_async_copy(f_ref, xa.at[own], loc.at[0])
    lc.start()
    ex = [cps.go(f_ref, xa.at[own], d) for _, d in plane]
    sib = weight_tail(p, cps, (wg, wu, wd), 4)
    for cp in ex + sib:
        cp.wait_recv()
    lc.wait()
    cps.drain_sends()


def scatter_plane(y_ref, rx, send, recv):
    p = Place()
    plane = [p.plane(o) for o in range(1, 16)]
    barrier([d for _, d in plane])
    cps = Copies(send, recv)
    ex = [cps.go(y_ref.at[j], rx.at[i], d) for i, (j, d) in enumerate(plane)]
    for cp in ex:
        cp.wait_recv()
    cps.drain_sends()


def gather_rows(f_ref, xa, send, recv, loc):
    p = Place()
    tens = [p.tens(o) for o in range(1, 8)]
    barrier([d for _, d in tens])
    cps = Copies(send, recv)
    lc = pltpu.make_async_copy(f_ref, xa.at[p.t], loc.at[0])
    lc.start()
    ex = [cps.go(f_ref, xa.at[p.t], d) for _, d in tens]
    for cp in ex:
        cp.wait_recv()
    lc.wait()
    cps.drain_sends()


def call(body, cid, ins, in_specs, outs, out_specs, n, n_loc=0, aliases=None):
    scratch = [pltpu.SemaphoreType.DMA((n,)), pltpu.SemaphoreType.DMA((n,))]
    if n_loc:
        scratch.append(pltpu.SemaphoreType.DMA((n_loc,)))
    return pl.pallas_call(
        body,
        out_shape=[jax.ShapeDtypeStruct(s, bf16) for s in outs],
        in_specs=in_specs,
        out_specs=out_specs,
        scratch_shapes=scratch,
        input_output_aliases=aliases or {},
        compiler_params=pltpu.CompilerParams(collective_id=cid, has_side_effects=True),
        name=body.__name__,
    )(*ins)


def attend(flags, sel, qa, kv, qinfo, ktag, out, acc, den):
    for qb in range(4):
        x, blk = qb // 2, qb % 2
        rows = pl.ds(blk * 128, 128)
        acc[...] = jnp.zeros_like(acc)
        den[...] = jnp.zeros_like(den)

        def step(k, carry):
            @pl.when(flags[qb * 16 + k] != 0)
            def _():
                qt = jnp.concatenate([qa[2 * x, rows, :], qa[2 * x + 1, rows, :]], axis=0)
                score = lax.dot_general(qt, kv[0, k], (((1,), (1,)), ((), ())), preferred_element_type=f32)
                capped = SOFT_CAP * jnp.tanh(score * (0.0625 / SOFT_CAP))
                tag = qinfo[0, pl.ds(x * 256 + blk * 128, 128), :]
                start = qinfo[1, pl.ds(x * 256 + blk * 128, 128), :]
                kt = ktag[k]
                ok = (kt <= tag) & (kt >= start)
                weight = jnp.exp(capped)
                weight = jnp.concatenate(
                    [jnp.where(ok, weight[:128], 0.0), jnp.where(ok, weight[128:], 0.0)], axis=0
                ).astype(bf16)
                den[...] += weight.astype(f32)
                acc[...] += jnp.dot(weight, kv[1, k], preferred_element_type=f32)
            return carry

        lax.fori_loop(0, 16, step, 0)
        total = jnp.sum(den[...], axis=1, keepdims=True)
        high = total.astype(bf16).astype(f32)
        lane = lax.broadcasted_iota(jnp.int32, (256, 128), 1)
        both = jnp.where(lane < 64, high, total - high).astype(bf16)
        num = acc[...].astype(bf16)
        for h in range(2):
            out[2 * x + h, rows, 0:256] = num[h * 128:(h + 1) * 128]
            out[2 * x + h, rows, 256:384] = both[h * 128:(h + 1) * 128]
    for x in range(2):
        for j in range(2):
            k = sel[x * 2 + j]
            keep = jnp.where(k >= 0, 1.0, 0.0)
            at = jnp.maximum(k, 0)
            for part in range(2):
                picked = jnp.where(keep > 0, kv[part, at].astype(f32), 0.0)
                out[2 * x + part, pl.ds(j * 128, 128), 384:640] = picked.astype(bf16)


def row_norm(values, gain_vec):
    values = values.astype(f32)
    scale_vec = lax.rsqrt(jnp.mean(values * values, axis=-1, keepdims=True) + EPS)
    return values * scale_vec * gain_vec


def starts_of(tags, lengths):
    e0 = lengths[0]
    e1 = e0 + lengths[1]
    e2 = e1 + lengths[2]
    return jnp.where(tags >= e2, e2, jnp.where(tags >= e1, e1, jnp.where(tags >= e0, e0, 0)))


def spin(values, cosine, sine):
    half_dim = values.shape[-1] // 2
    a = values[:, :half_dim]
    b = values[:, half_dim:]
    return jnp.concatenate([a * cosine - b * sine, b * cosine + a * sine], axis=1)


def body(
    hidden, attn_gain, query_weight, kv_weight, out_weight, post_gain, ff_gain, ff_post_gain,
    gate_weight, up_weight, down_weight_t, next_gain, next_query_weight, next_kv_weight,
    lengths, pair_owner, page_table,
):
    p = Place()
    is_key = p.yb == 0
    local = jnp.arange(128, dtype=jnp.int32)
    ids = jnp.arange(32, dtype=jnp.int32)

    def pairs(idx):
        return jnp.sum(jnp.where(ids[None, :] == idx[:, None], pair_owner[None, :], 0), axis=1)

    qs = jnp.stack([p.z * 2 + p.c, 16 + p.z * 2 + p.c])
    qpair = pairs(qs)
    qblock = jnp.stack([qpair, 63 - qpair], axis=1).reshape(4)
    qtags = (qblock[:, None] * 128 + local[None, :]).reshape(512)
    qstart = starts_of(qtags, lengths)
    qinfo = jnp.stack([qtags, qstart])[:, :, None]
    kpair = pairs(p.x * 16 + jnp.arange(16, dtype=jnp.int32))
    kblock = jnp.where(is_key, kpair, 63 - kpair)
    ktag = (kblock[:, None] * 128 + local[None, :])[:, None, :]
    qfirst = starts_of(qblock * 128, lengths)
    flags = ((kblock[None, :] <= qblock[:, None]) & (kblock[None, :] * 128 + 127 >= qfirst[:, None])).astype(jnp.int32).reshape(64)
    pages = (2 * qs[:, None] + jnp.arange(2, dtype=jnp.int32)[None, :]).reshape(4)
    wanted = jnp.sum(jnp.where(page_table[None, :] == pages[:, None], jnp.arange(64, dtype=jnp.int32)[None, :], 0), axis=1)
    sel = jnp.sum(jnp.where(kblock[None, :] == wanted[:, None], jnp.arange(1, 17, dtype=jnp.int32)[None, :], 0), axis=1) - 1

    tags = lax.dynamic_slice_in_dim(qtags, p.x * 256, 256, 0)
    position = tags - lax.dynamic_slice_in_dim(qstart, p.x * 256, 256, 0)
    freq_vec = 10000.0 ** (-jnp.arange(128, dtype=f32) / 128)
    angles = position.astype(f32)[:, None] * freq_vec[None, :]
    cosine, sine = jnp.cos(angles), jnp.sin(angles)

    wshape = (2, 16, 72, FFP)
    xt, wg, wu, wd = call(
        gather_hidden, 1, (hidden.T, gate_weight, up_weight, down_weight_t), [VM] * 4,
        [(2304, 256), wshape, wshape, wshape], [VM, AN, AN, AN], 32, 4,
    )
    full_hidden = xt.T
    attn_input = row_norm(full_hidden, attn_gain).astype(bf16)
    queries = spin(jnp.dot(attn_input, query_weight, preferred_element_type=f32), cosine, sine).astype(bf16)
    own_proj = jnp.dot(attn_input, kv_weight, preferred_element_type=f32)
    own_part = jnp.where(is_key, spin(own_proj, cosine, sine), own_proj).astype(bf16)
    stay = jnp.where(is_key, own_part[:128], own_part[128:])
    go = jnp.where(is_key, own_part[128:], own_part[:128])
    kv, qa = call(
        exchange_kv, 2, (stay, go, queries), [VM] * 3, [(2, 16, 128, 256), (4, 256, 256)], [VM, VM], 24, 2,
    )
    part = pl.pallas_call(
        attend,
        out_shape=jax.ShapeDtypeStruct((4, 256, 640), bf16),
        in_specs=[pl.BlockSpec(memory_space=pltpu.SMEM)] * 2 + [VM] * 4,
        out_specs=VM,
        scratch_shapes=[pltpu.VMEM((256, 256), f32), pltpu.VMEM((256, 128), f32)],
        name="attend",
    )(flags, sel, qa, kv, qinfo, ktag)
    rx, wg, wu, wd = call(
        exchange_partials, 3, (part, wg, wu, wd), [VM, AN, AN, AN],
        [(3, 256, 640), wshape, wshape, wshape], [VM, AN, AN, AN], 16, 0, {1: 1, 2: 2, 3: 3},
    )
    mine = lax.dynamic_index_in_dim(part, p.x * 2 + p.yb, 0, keepdims=False).astype(f32)
    whole = mine + rx[0].astype(f32) + rx[1].astype(f32) + rx[2].astype(f32)
    kv_pages = whole[:, 384:640].astype(bf16).reshape(2, 128, 256)
    denominator = jnp.sum(whole[:, 256:384], axis=1, keepdims=True) * (1.0 / 64)
    attended = (whole[:, :256] / denominator).astype(bf16)
    partial = jnp.dot(attended, out_weight, preferred_element_type=f32).astype(bf16).reshape(8, 32, 2304)
    rx, wg, wu, wd = call(
        scatter_tensor, 4, (partial, wg, wu, wd), [VM, AN, AN, AN],
        [(7, 32, 2304), wshape, wshape, wshape], [VM, AN, AN, AN], 20, 0, {1: 1, 2: 2, 3: 3},
    )
    mine = lax.dynamic_index_in_dim(partial, p.t, 0, keepdims=False).astype(f32)
    attn_sum = mine + jnp.sum(rx.astype(f32), axis=0)
    own_hidden = lax.dynamic_slice_in_dim(full_hidden, p.t * 32, 32, 0).astype(f32)
    middle = (own_hidden + row_norm(attn_sum, post_gain)).astype(bf16)
    ff_input = row_norm(middle, ff_gain).astype(bf16)
    xa, wg, wu, wd = call(
        gather_plane, 5, (ff_input, wg, wu, wd), [VM, AN, AN, AN],
        [(16, 32, 2304), wshape, wshape, wshape], [VM, AN, AN, AN], 26, 1, {1: 1, 2: 2, 3: 3},
    )
    rows = xa.reshape(512, 2304)
    gate_val = jnp.dot(rows, wg.reshape(2304, FFP), preferred_element_type=f32)
    up_val = jnp.dot(rows, wu.reshape(2304, FFP), preferred_element_type=f32)
    column = jnp.arange(FFP, dtype=jnp.int32)
    keep = (p.x == 0) | (column >= FFP - FFO)
    inner = jnp.where(keep[None, :], jax.nn.gelu(gate_val, approximate=True) * up_val, 0.0).astype(bf16)
    ff_partial = lax.dot_general(
        inner, wd.reshape(2304, FFP), (((1,), (1,)), ((), ())), preferred_element_type=f32
    ).astype(bf16).reshape(16, 32, 2304)
    (rx,) = call(scatter_plane, 6, (ff_partial,), [VM], [(15, 32, 2304)], [VM], 15)
    mine = lax.dynamic_index_in_dim(ff_partial, p.x * 8 + p.t, 0, keepdims=False).astype(f32)
    ff_sum = mine + jnp.sum(rx.astype(f32), axis=0)
    own_final = (middle.astype(f32) + row_norm(ff_sum, ff_post_gain)).astype(bf16)
    (fr,) = call(gather_rows, 7, (own_final,), [VM], [(8, 32, 2304)], [VM], 7, 1)
    final_rows = fr.reshape(256, 2304)
    next_input = row_norm(final_rows, next_gain).astype(bf16)
    hidden_out = lax.dynamic_slice_in_dim(final_rows, p.t * 288, 288, 1)
    next_query = spin(jnp.dot(next_input, next_query_weight, preferred_element_type=f32), cosine, sine).astype(bf16)
    next_proj = jnp.dot(next_input, next_kv_weight, preferred_element_type=f32)
    next_kv = jnp.where(is_key, spin(next_proj, cosine, sine), next_proj).astype(bf16)
    return (hidden_out, next_query, next_kv, kv_pages)


def solution(mesh):
    wide = P("seq", "tensor")
    cols = P(None, "tensor")
    in_specs = (wide, P(), cols, cols, P("tensor", None), P(), P(), P(), wide, wide, wide, P(), cols, cols, P(), P(), P())
    out_specs = (wide, wide, wide, P("seq", None, "tensor"))
    return jax.shard_map(body, mesh=mesh, in_specs=in_specs, out_specs=out_specs, check_vma=False)
```

```python
import functools

import jax
import jax.numpy as jnp
from jax import lax
from jax.experimental import pallas as pl
from jax.experimental.pallas import tpu as pltpu
from jax.sharding import PartitionSpec as P

EPS = 1e-06
SOFT_CAP = 50.0
MESH = pl.DeviceIdType.MESH
VM = pl.BlockSpec(memory_space=pltpu.VMEM)
AN = pl.BlockSpec(memory_space=pl.ANY)
FFP = 640
FFO = 512
bf16 = jnp.bfloat16
f32 = jnp.float32


class Place:
    def __init__(self):
        self.s = lax.axis_index("seq")
        self.t = lax.axis_index("tensor")
        self.x = self.s // 16
        self.z = (self.s // 2) % 8
        self.c = self.s % 2
        self.yb = self.t % 2
        self.X = self.x * 2 + self.t // 4
        self.Y = self.t % 4

    def grid(self, X, Y):
        return self.dev(self.seq(X // 2, self.z, self.c), (X % 2) * 4 + Y)

    def near(self, dim, sign, nx):
        if dim == 1:
            return self.grid(self.X, (self.Y + 4 + sign) % 4)
        if nx == 2:
            return self.dev(self.s, (self.t + 4) % 8)
        return self.grid((self.X + 4 + sign) % 4, self.Y)

    def around(self, nx):
        out = [self.near(1, 1, nx), self.near(1, -1, nx), self.near(0, 1, nx)]
        return out + ([self.near(0, -1, nx)] if nx == 4 else [])

    def seq(self, x, z, c):
        return x * 16 + z * 2 + c

    def dev(self, s, t):
        return {"seq": s, "tensor": t}

    def zp(self):
        return self.dev(self.seq(self.x, (self.z + 1) % 8, self.c), self.t)

    def zm(self):
        return self.dev(self.seq(self.x, (self.z + 7) % 8, self.c), self.t)

    def sib(self):
        return self.dev(self.seq(self.x, self.z, 1 - self.c), self.t)

    def xpart(self):
        return self.dev(self.seq(1 - self.x, self.z, self.c), self.t)

    def quad(self, o):
        dx, dy = o // 2, o % 2
        x = (self.x + dx) % 2
        yb = (self.yb + dy) % 2
        return x, yb, self.dev(self.seq(x, self.z, self.c), self.t - self.yb + yb)

    def tens(self, o):
        t = (self.t + o) % 8
        return t, self.dev(self.s, t)

    def plane(self, o):
        j = (self.x * 8 + self.t + o) % 16
        x, t = j // 8, j % 8
        return j, self.dev(self.seq(x, self.z, self.c), t)


class Copies:
    def __init__(self, send, recv):
        self.send, self.recv, self.n, self.live = send, recv, 0, []

    def make(self, src, dst, dev):
        i = self.n
        self.n += 1
        return pltpu.make_async_remote_copy(
            src_ref=src, dst_ref=dst, send_sem=self.send.at[i], recv_sem=self.recv.at[i],
            device_id=dev, device_id_type=MESH,
        )

    def go(self, src, dst, dev):
        cp = self.make(src, dst, dev)
        cp.start()
        self.live.append(cp)
        return cp

    def drain_sends(self):
        for cp in self.live:
            cp.wait_send()


def barrier(peers):
    sem = pltpu.get_barrier_semaphore()
    for dev in peers:
        pl.semaphore_signal(sem, inc=1, device_id=dev, device_id_type=MESH)
    pl.semaphore_wait(sem, len(peers))


def gather_grid(p, cps, own, view, nx):
    size = (nx, 4)

    def send(h, a, b, sub, dim, sign):
        dx, dy = (a, b) if h == 0 else (b, a)
        dst = view(dx, dy, h, sub)
        return cps.go(own(h) if (a, b) == (0, 0) else dst, dst, p.near(dim, sign, nx))

    def spread(h, a, b, dim):
        return [send(h, a, b, None, dim, sign) for sign in ((1, -1) if size[dim] == 4 else (1,))]

    first = [spread(h, 0, 0, h) for h in range(2)]
    second = [{0: spread(h, 0, 0, 1 - h)} for h in range(2)]
    far = [[], []]
    last = []
    for i in range(2):
        for h in range(2):
            if i < len(first[h]):
                first[h][i].wait_recv()
                a = (-1, 1)[i]
                if size[h] == 4:
                    far[h].append(send(h, a, 0, i, h, -a))
                second[h][a] = spread(h, a, 0, 1 - h)

    def onward(h, a):
        for i, cp in enumerate(second[h][a]):
            cp.wait_recv()
            if size[1 - h] == 4:
                b = (-1, 1)[i]
                last.append(send(h, a, b, i, 1 - h, -b))

    for h in range(2):
        onward(h, 0)
    for h in range(2):
        if far[h]:
            for cp in far[h]:
                cp.wait_recv()
            second[h][2] = spread(h, 2, 0, 1 - h)
    for a in (-1, 1, 2):
        for h in range(2):
            if a in second[h]:
                onward(h, a)
    for cp in last:
        cp.wait_recv()


ROW = (slice(0, 16), slice(16, 32))
COL = (slice(0, 1152), slice(1152, 2304))


def reduce_line(p, cps, read, view, buf, dim, nx):
    size = (nx, 4)[dim]
    rp, rm, up, dn, bu, bd = buf
    plus, minus = p.near(dim, 1, nx), p.near(dim, -1, nx)
    if size == 2:
        cp = cps.go(view(1, None), rp, plus)

        def finish():
            cp.wait_recv()
            return read(0, None) + rp[...].astype(f32)

        return [finish]
    far0 = cps.go(view(2, 0), up, plus)
    far1 = cps.go(view(2, 1), dn, minus)
    near = [cps.go(view(1, 1), rp.at[:, ROW[1]], plus), cps.go(view(-1, 0), rm.at[:, ROW[0]], minus)]

    def relay():
        far0.wait_recv()
        bu[...] = (read(1, 0) + up[...].astype(f32)).astype(bf16)
        near.append(cps.go(bu, rp.at[:, ROW[0]], plus))
        far1.wait_recv()
        bd[...] = (read(-1, 1) + dn[...].astype(f32)).astype(bf16)
        near.append(cps.go(bd, rm.at[:, ROW[1]], minus))

    def finish():
        for cp in near:
            cp.wait_recv()
        return read(0, None) + rp[...].astype(f32) + rm[...].astype(f32)

    return [relay, finish]


def reduce_grid(p, cps, part, bufs, sums, nx):
    at = (p.X if nx == 4 else p.X % 2, p.Y)
    size = (nx, 4)

    def one(h):
        def view(d, sub):
            rows = slice(0, 32) if sub is None else ROW[sub]
            i = (at[1 - h] + size[1 - h] + d) % size[1 - h]
            return part.at[:, i, rows, COL[h]] if h == 0 else part.at[i, :, rows, COL[h]]

        def read(d, sub):
            return view(d, sub)[...].astype(f32)

        return reduce_line(p, cps, read, view, bufs[h][:6], 1 - h, nx)

    def two(h):
        def view(d, sub):
            rows = slice(0, 32) if sub is None else ROW[sub]
            i = (at[h] + size[h] + d) % size[h]
            return sums[h].at[pl.ds(i, 1), rows]

        def read(d, sub):
            return view(d, sub)[...].astype(f32)

        return reduce_line(p, cps, read, view, bufs[h][6:], h, nx)

    steps = [one(h) for h in range(2)]
    for h in range(2):
        if len(steps[h]) == 2:
            steps[h][0]()
    later = []
    for h in range(2):
        sums[h][...] = steps[h][-1]().astype(bf16)
        later.append(two(h))
    for h in range(2):
        if len(later[h]) == 2:
            later[h][0]()
    return [later[h][-1]()[0] for h in range(2)]


def reduce_scratch(nx):
    out = []
    for h in range(2):
        size = (nx, 4)
        for n, m in ((size[h], size[1 - h]), (1, size[h])):
            del m
            out += [pltpu.VMEM((n, 32, 1152), bf16)] * 2 + [pltpu.VMEM((n, 16, 1152), bf16)] * 4
        out.append(pltpu.VMEM((size[h], 32, 1152), bf16))
    return out


def reduce_bufs(refs):
    return [refs[0:12], refs[13:25]], [refs[12], refs[25]]


def normed(values, gain):
    return values * lax.rsqrt(jnp.mean(values * values, axis=1, keepdims=True) + EPS) * gain[...]


def weight_round(p, cps, ws, d):
    got = []
    right = ((p.z + 9 - d) % 8) * 2 + p.c
    left = ((p.z + 7 + d) % 8) * 2 + p.c
    for w in ws:
        if d < 4:
            got.append((cps.go(w.at[:, right], w.at[:, right], p.zp()), w))
            got.append((cps.go(w.at[:, left], w.at[:, left], p.zm()), w))
        else:
            got.append((cps.go(w.at[0, right], w.at[0, right], p.zp()), w))
            got.append((cps.go(w.at[1, left], w.at[1, left], p.zm()), w))
    return got


def weight_finish(p, cps, got, d):
    right = ((p.z + 8 - d) % 8) * 2 + p.c
    left = ((p.z + d) % 8) * 2 + p.c
    out = []
    for i, (cp, w) in enumerate(got):
        cp.wait_recv()
        if d < 4:
            slot = right if i % 2 == 0 else left
            out.append(cps.go(w.at[:, slot], w.at[:, slot], p.sib()))
        elif i % 2 == 1:
            out.append(cps.go(w.at[:, right], w.at[:, right], p.sib()))
    return out


def gather_hidden(ht, gate, up, down, xt, wg, wu, wd, send, recv, loc):
    p = Place()
    barrier(p.around(2) + [p.xpart(), p.zp(), p.zm(), p.sib()])
    cps = Copies(send, recv)
    ws = (wg, wu, wd)
    slot = p.z * 2 + p.c
    mine = pl.ds(pl.multiple_of(p.x * FFO, 128), FFP)
    other = pl.ds(pl.multiple_of((1 - p.x) * FFO, 128), FFP)
    swaps = [cps.go(a.at[:, other], w.at[p.x, slot], p.xpart()) for a, w in zip((gate, up, down), ws)]
    ring = [cps.go(a.at[:, mine], w.at[p.x, slot], dev) for a, w in zip((gate, up, down), ws)
            for dev in (p.zp(), p.zm())]
    locs = [pltpu.make_async_copy(a.at[:, mine], w.at[p.x, slot], loc.at[i])
            for i, (a, w) in enumerate(zip((gate, up, down), ws))]

    def view(dx, dy, h, sub):
        t = ((p.t // 4 + 2 + dx) % 2) * 4 + (p.Y + 4 + dy) % 4
        low, n = ((0, 144) if sub is None else ((0, 80), (80, 64))[sub])
        return xt.at[t, pl.ds(h * 144 + low, n)]

    locs.append(pltpu.make_async_copy(ht, xt.at[p.t], loc.at[3]))
    for cp in locs:
        cp.start()
    gather_grid(p, cps, lambda h: ht.at[pl.ds(h * 144, 144)], view, 2)
    for cp in swaps:
        cp.wait_recv()
    for w in ws:
        ring += [cps.go(w.at[1 - p.x, slot], w.at[1 - p.x, slot], dev) for dev in (p.zp(), p.zm())]
    for cp in locs:
        cp.wait()
    sib = [cps.go(w.at[:, slot], w.at[:, slot], p.sib()) for w in ws]
    right = ((p.z + 7) % 8) * 2 + p.c
    left = ((p.z + 1) % 8) * 2 + p.c
    for i in range(6):
        ring[i].wait_recv()
        ring[i + 6].wait_recv()
        w = ws[i // 2]
        at = right if i % 2 == 0 else left
        sib.append(cps.go(w.at[:, at], w.at[:, at], p.sib()))
    for cp in sib:
        cp.wait_recv()
    cps.drain_sends()


def exchange_kv(stay, go, q, kv, qa, send, recv, loc):
    p = Place()
    quads = [p.quad(o) for o in range(1, 4)]
    barrier([d for _, _, d in quads] + [p.zp(), p.zm(), p.sib()])
    cps = Copies(send, recv)
    slot = p.z * 2 + p.c
    parts = (p.yb, 1 - p.yb)
    pair = cps.go(go, kv.at[p.yb, slot], quads[0][2])
    got = [[cps.go(stay, kv.at[p.yb, slot], p.zp()), cps.go(stay, kv.at[p.yb, slot], p.zm())]]
    locs = [pltpu.make_async_copy(stay, kv.at[p.yb, slot], loc.at[0]),
            pltpu.make_async_copy(q, qa.at[p.x * 2 + p.yb], loc.at[1])]
    for cp in locs:
        cp.start()
    sib = [cps.go(stay, kv.at[p.yb, slot], p.sib())]
    qs = [cps.go(q, qa.at[p.x * 2 + p.yb], d) for _, _, d in quads]
    pair.wait_recv()
    own = kv.at[1 - p.yb, slot]
    got.append([cps.go(own, own, p.zp()), cps.go(own, own, p.zm())])
    sib.append(cps.go(own, own, p.sib()))
    for d in range(1, 5):
        right = ((p.z + 8 - d) % 8) * 2 + p.c
        left = ((p.z + d) % 8) * 2 + p.c
        nxt = [[], []]
        for i, part in enumerate(parts):
            for side, cp in enumerate(got[i]):
                cp.wait_recv()
                if d < 4:
                    here = kv.at[part, (right, left)[side]]
                    if d < 3 or side == i:
                        nxt[i].append(cps.go(here, here, (p.zp(), p.zm())[side]))
                    sib.append(cps.go(here, here, p.sib()))
                else:
                    here = kv.at[part, right]
                    sib.append(cps.go(here, here, p.sib()))
        got = nxt
    for cp in locs:
        cp.wait()
    for cp in qs + sib:
        cp.wait_recv()
    cps.drain_sends()


def exchange_partials(num, den, wg0, wu0, wd0, rn, rd, wg, wu, wd, send, recv):
    p = Place()
    quads = [p.quad(o) for o in range(1, 4)]
    barrier([d for _, _, d in quads] + [p.zp(), p.zm(), p.sib()])
    cps = Copies(send, recv)
    ex = [cps.go(num.at[x * 2 + yb], rn.at[o], d) for o, (x, yb, d) in enumerate(quads)]
    ex += [cps.go(den.at[x * 2 + yb], rd.at[o], d) for o, (x, yb, d) in enumerate(quads)]
    got = weight_round(p, cps, (wg, wu, wd), 2)
    sib = weight_finish(p, cps, got, 2)
    for cp in ex + sib:
        cp.wait_recv()
    cps.drain_sends()


def mix_tensor(o_ref, hid, post_gain, ff_gain, wg0, wu0, wd0, mid, xa, wg, wu, wd, send, recv, loc, mine, *scratch):
    p = Place()
    barrier(p.around(4) + [p.zp(), p.zm(), p.sib()])
    cps = Copies(send, recv)
    ws = (wg, wu, wd)
    got = weight_round(p, cps, ws, 3)
    bufs, sums = reduce_bufs(scratch)
    total = jnp.concatenate(reduce_grid(p, cps, o_ref, bufs, sums, 2), axis=1)
    middle = (hid[...].astype(f32) + normed(total, post_gain)).astype(bf16)
    mid[...] = middle
    mine[...] = normed(middle.astype(f32), ff_gain).astype(bf16)
    lc = pltpu.make_async_copy(mine, xa.at[p.X, p.Y], loc.at[0])
    lc.start()
    sib = weight_finish(p, cps, got, 3)
    got = weight_round(p, cps, ws, 4)

    def view(dx, dy, h, sub):
        rows = slice(0, 32) if sub is None else ROW[sub]
        return xa.at[(p.X + 4 + dx) % 4, (p.Y + 4 + dy) % 4, rows, COL[h]]

    gather_grid(p, cps, lambda h: mine.at[:, COL[h]], view, 4)
    sib += weight_finish(p, cps, got, 4)
    for cp in sib:
        cp.wait_recv()
    lc.wait()
    cps.drain_sends()


def mix_plane(y_ref, mid, gain, xa, send, recv, loc, mine, *scratch):
    p = Place()
    barrier(p.around(4))
    cps = Copies(send, recv)
    bufs, sums = reduce_bufs(scratch)
    total = jnp.concatenate(reduce_grid(p, cps, y_ref, bufs, sums, 4), axis=1)
    mine[...] = (mid[...].astype(f32) + normed(total, gain)).astype(bf16)
    lc = pltpu.make_async_copy(mine, xa.at[p.t], loc.at[0])
    lc.start()

    def view(dx, dy, h, sub):
        rows = slice(0, 32) if sub is None else ROW[sub]
        return xa.at[((p.X + 2 + dx) % 2) * 4 + (p.Y + 4 + dy) % 4, rows, COL[h]]

    gather_grid(p, cps, lambda h: mine.at[:, COL[h]], view, 2)
    lc.wait()
    cps.drain_sends()


def call(body, cid, ins, in_specs, outs, out_specs, n, n_loc=0, aliases=None, extra=()):
    scratch = [pltpu.SemaphoreType.DMA((n,)), pltpu.SemaphoreType.DMA((n,))]
    if n_loc:
        scratch.append(pltpu.SemaphoreType.DMA((n_loc,)))
    return pl.pallas_call(
        body,
        out_shape=[s if isinstance(s, jax.ShapeDtypeStruct) else jax.ShapeDtypeStruct(s, bf16) for s in outs],
        in_specs=in_specs,
        out_specs=out_specs,
        scratch_shapes=scratch + list(extra),
        input_output_aliases=aliases or {},
        compiler_params=pltpu.CompilerParams(collective_id=cid, has_side_effects=True),
        name=body.__name__,
    )(*ins)


def attend(lengths, owner, table, qa, kv, out, out_den, out_page, acc, den):
    p = Place()
    e0 = lengths[0]
    e1 = e0 + lengths[1]
    e2 = e1 + lengths[2]

    def start_of(tag):
        return jnp.where(tag >= e2, e2, jnp.where(tag >= e1, e1, jnp.where(tag >= e0, e0, 0)))

    row = lax.broadcasted_iota(jnp.int32, (128, 128), 0)
    lane = lax.broadcasted_iota(jnp.int32, (128, 128), 1)

    def key_block(k):
        b = owner[p.x * 16 + k]
        return jnp.where(p.yb == 0, b, 63 - b)

    for qb in range(4):
        x, blk = qb // 2, qb % 2
        rows = pl.ds(blk * 128, 128)
        acc[...] = jnp.zeros_like(acc)
        den[...] = jnp.zeros_like(den)
        b = owner[x * 16 + p.z * 2 + p.c]
        q_block = b if blk == 0 else 63 - b
        first = start_of(q_block * 128)

        def step(k, carry):
            k_block = key_block(k)

            @pl.when((k_block <= q_block) & (k_block * 128 + 127 >= first))
            def _():
                qt = jnp.concatenate([qa[2 * x, rows, :], qa[2 * x + 1, rows, :]], axis=0)
                score = lax.dot_general(qt, kv[0, k], (((1,), (1,)), ((), ())), preferred_element_type=f32)
                capped = SOFT_CAP * jnp.tanh(score * (0.0625 / SOFT_CAP))
                tag = q_block * 128 + row
                kt = k_block * 128 + lane
                ok = (kt <= tag) & (kt >= start_of(tag))
                weight = jnp.exp(capped)
                weight = jnp.concatenate(
                    [jnp.where(ok, weight[:128], 0.0), jnp.where(ok, weight[128:], 0.0)], axis=0
                ).astype(bf16)
                den[...] += weight.astype(f32)
                acc[...] += jnp.dot(weight, kv[1, k], preferred_element_type=f32)
            return carry

        lax.fori_loop(0, 16, step, 0)
        total = lax.dot_general(
            jnp.ones((8, 128), f32), den[...], (((1,), (1,)), ((), ())),
            precision=lax.Precision.HIGHEST, preferred_element_type=f32,
        )
        num = acc[...].astype(bf16)
        for h in range(2):
            out[2 * x + h, rows, :] = num[h * 128:(h + 1) * 128]
            out_den[2 * x + h, :, blk * 128:(blk + 1) * 128] = total[:, h * 128:(h + 1) * 128]

    base = p.z * 4 + p.c * 2

    def look(i, found):
        page = table[i]
        return tuple(jnp.where(page == (n // 2) * 32 + base + n % 2, i, f) for n, f in enumerate(found))

    wanted = lax.fori_loop(0, 64, look, (jnp.int32(0),) * 4)

    def match(k, found):
        block = key_block(k)
        return tuple(jnp.where(block == w, k, f) for w, f in zip(wanted, found))

    chosen = lax.fori_loop(0, 16, match, (jnp.int32(-1),) * 4)
    for n in range(4):
        at = jnp.maximum(chosen[n], 0)
        for part in range(2):
            picked = jnp.where(chosen[n] >= 0, kv[part, at].astype(f32), 0.0)
            out_page[(n // 2) * 2 + part, pl.ds((n % 2) * 128, 128), :] = picked.astype(bf16)


def quad_route(dx, dy):
    route = []
    for s in range(32):
        for t in range(8):
            route.append((s * 8 + t, ((s + 16 * dx) % 32) * 8 + (t ^ dy)))
    return route


def row_norm(values, gain_vec):
    values = values.astype(f32)
    scale_vec = lax.rsqrt(jnp.mean(values * values, axis=-1, keepdims=True) + EPS)
    return values * scale_vec * gain_vec


def starts_of(tags, lengths):
    e0 = lengths[0]
    e1 = e0 + lengths[1]
    e2 = e1 + lengths[2]
    return jnp.where(tags >= e2, e2, jnp.where(tags >= e1, e1, jnp.where(tags >= e0, e0, 0)))


def spin(values, cosine, sine):
    half_dim = values.shape[-1] // 2
    a = values[:, :half_dim]
    b = values[:, half_dim:]
    return jnp.concatenate([a * cosine - b * sine, b * cosine + a * sine], axis=1)


def body(
    hidden, attn_gain, query_weight, kv_weight, out_weight, post_gain, ff_gain, ff_post_gain,
    gate_weight, up_weight, down_weight_t, next_gain, next_query_weight, next_kv_weight,
    lengths, pair_owner, page_table,
):
    p = Place()
    is_key = p.yb == 0
    owned = jnp.sum(jnp.where(jnp.arange(32, dtype=jnp.int32) == p.s, pair_owner, 0))
    local = jnp.arange(256, dtype=jnp.int32)
    tags = jnp.where(local < 128, owned * 128 + local, (63 - owned) * 128 + local - 128)
    position = tags - starts_of(tags, lengths)
    freq_vec = 10000.0 ** (-jnp.arange(128, dtype=f32) / 128)
    angles = position.astype(f32)[:, None] * freq_vec[None, :]
    cosine, sine = jnp.cos(angles), jnp.sin(angles)

    wshape = (2, 16, 72, FFP)
    xt, wg, wu, wd = call(
        gather_hidden, 1, (hidden.T, gate_weight, up_weight, down_weight_t), [VM] * 4,
        [(8, 288, 256), wshape, wshape, wshape], [VM, AN, AN, AN], 64, 4,
    )
    full_hidden = xt.reshape(2304, 256).T
    attn_input = row_norm(full_hidden, attn_gain).astype(bf16)
    queries = spin(jnp.dot(attn_input, query_weight, preferred_element_type=f32), cosine, sine).astype(bf16)
    own_proj = jnp.dot(attn_input, kv_weight, preferred_element_type=f32)
    own_part = jnp.where(is_key, spin(own_proj, cosine, sine), own_proj).astype(bf16)
    stay = jnp.where(is_key, own_part[:128], own_part[128:])
    go = jnp.where(is_key, own_part[128:], own_part[:128])
    kv, qa = call(
        exchange_kv, 2, (stay, go, queries), [VM] * 3, [(2, 16, 128, 256), (4, 256, 256)], [VM, VM], 40, 2,
    )
    num, den, page = pl.pallas_call(
        attend,
        out_shape=[jax.ShapeDtypeStruct((4, 256, 256), bf16), jax.ShapeDtypeStruct((4, 8, 256), f32),
                   jax.ShapeDtypeStruct((4, 256, 256), bf16)],
        in_specs=[pl.BlockSpec(memory_space=pltpu.SMEM)] * 3 + [VM] * 2,
        out_specs=[VM] * 3,
        scratch_shapes=[pltpu.VMEM((256, 256), f32), pltpu.VMEM((256, 128), f32)],
        name="attend",
    )(lengths, pair_owner, page_table, qa, kv)
    spot = p.x * 2 + p.yb

    def pick(a, i):
        return lax.dynamic_index_in_dim(a, i, 0, keepdims=False)

    rn, rd, wg, wu, wd = call(
        exchange_partials, 3, (num, den, wg, wu, wd), [VM, VM, AN, AN, AN],
        [(3, 256, 256), jax.ShapeDtypeStruct((3, 8, 256), f32), wshape, wshape, wshape],
        [VM, VM, AN, AN, AN], 20, 0, {2: 2, 3: 3, 4: 4},
    )
    pages = pick(page, spot).astype(f32)
    for o in range(1, 4):
        dx, dy = o // 2, o % 2
        peer = ((p.x + dx) % 2) * 2 + (p.yb + dy) % 2
        pages += lax.ppermute(pick(page, peer), ("seq", "tensor"), quad_route(dx, dy)).astype(f32)
    kv_pages = pages.astype(bf16).reshape(2, 128, 256)
    numerator = pick(num, spot).astype(f32) + rn[0].astype(f32) + rn[1].astype(f32) + rn[2].astype(f32)
    denominator = (pick(den, spot) + rd[0] + rd[1] + rd[2])[0][:, None]
    attended = (numerator / denominator).astype(bf16)
    partial = jnp.dot(attended, out_weight, preferred_element_type=f32).astype(bf16).reshape(2, 4, 32, 2304)
    own_hidden = lax.dynamic_slice_in_dim(full_hidden, p.t * 32, 32, 0)
    mine = pltpu.VMEM((32, 2304), bf16)
    middle, xa, wg, wu, wd = call(
        mix_tensor, 4, (partial, own_hidden, post_gain[None, :], ff_gain[None, :], wg, wu, wd), [VM] * 4 + [AN] * 3,
        [(32, 2304), (4, 4, 32, 2304), wshape, wshape, wshape], [VM, VM, AN, AN, AN], 100, 1,
        {4: 2, 5: 3, 6: 4}, [mine] + reduce_scratch(2),
    )
    rows = xa.reshape(512, 2304)
    gate_val = jnp.dot(rows, wg.reshape(2304, FFP), preferred_element_type=f32)
    up_val = jnp.dot(rows, wu.reshape(2304, FFP), preferred_element_type=f32)
    column = jnp.arange(FFP, dtype=jnp.int32)
    keep = (p.x == 0) | (column >= FFP - FFO)
    inner = jnp.where(keep[None, :], jax.nn.gelu(gate_val, approximate=True) * up_val, 0.0).astype(bf16)
    ff_partial = lax.dot_general(
        inner, wd.reshape(2304, FFP), (((1,), (1,)), ((), ())), preferred_element_type=f32
    ).astype(bf16).reshape(4, 4, 32, 2304)
    (fr,) = call(
        mix_plane, 5, (ff_partial, middle, ff_post_gain[None, :]), [VM] * 3, [(8, 32, 2304)], [VM], 60, 1, None,
        [mine] + reduce_scratch(4),
    )
    final_rows = fr.reshape(256, 2304)
    next_input = row_norm(final_rows, next_gain).astype(bf16)
    hidden_out = lax.dynamic_slice_in_dim(final_rows, p.t * 288, 288, 1)
    next_query = spin(jnp.dot(next_input, next_query_weight, preferred_element_type=f32), cosine, sine).astype(bf16)
    next_proj = jnp.dot(next_input, next_kv_weight, preferred_element_type=f32)
    next_kv = jnp.where(is_key, spin(next_proj, cosine, sine), next_proj).astype(bf16)
    return (hidden_out, next_query, next_kv, kv_pages)


def solution(mesh):
    wide = P("seq", "tensor")
    cols = P(None, "tensor")
    in_specs = (wide, P(), cols, cols, P("tensor", None), P(), P(), P(), wide, wide, wide, P(), cols, cols, P(), P(), P())
    out_specs = (wide, wide, wide, P("seq", None, "tensor"))
    return jax.shard_map(body, mesh=mesh, in_specs=in_specs, out_specs=out_specs, check_vma=False)
```

```python
import functools

import jax
import jax.numpy as jnp
from jax import lax
from jax.experimental import pallas as pl
from jax.experimental.pallas import tpu as pltpu
from jax.sharding import PartitionSpec as P

EPS = 1e-06
SOFT_CAP = 50.0
MESH = pl.DeviceIdType.MESH
VM = pl.BlockSpec(memory_space=pltpu.VMEM)
AN = pl.BlockSpec(memory_space=pl.ANY)
FFP = 640
FFO = 512
bf16 = jnp.bfloat16
f32 = jnp.float32


class Place:
    def __init__(self):
        self.s = lax.axis_index("seq")
        self.t = lax.axis_index("tensor")
        self.x = self.s // 16
        self.z = (self.s // 2) % 8
        self.c = self.s % 2
        self.yb = self.t % 2
        self.X = self.x * 2 + self.t // 4
        self.Y = self.t % 4

    def grid(self, X, Y):
        return self.dev(self.seq(X // 2, self.z, self.c), (X % 2) * 4 + Y)

    def near(self, dim, sign, nx):
        if dim == 1:
            return self.grid(self.X, (self.Y + 4 + sign) % 4)
        if nx == 2:
            return self.dev(self.s, (self.t + 4) % 8)
        return self.grid((self.X + 4 + sign) % 4, self.Y)

    def around(self, nx):
        out = [self.near(1, 1, nx), self.near(1, -1, nx), self.near(0, 1, nx)]
        return out + ([self.near(0, -1, nx)] if nx == 4 else [])

    def seq(self, x, z, c):
        return x * 16 + z * 2 + c

    def dev(self, s, t):
        return {"seq": s, "tensor": t}

    def zp(self):
        return self.dev(self.seq(self.x, (self.z + 1) % 8, self.c), self.t)

    def zm(self):
        return self.dev(self.seq(self.x, (self.z + 7) % 8, self.c), self.t)

    def sib(self):
        return self.dev(self.seq(self.x, self.z, 1 - self.c), self.t)

    def xpart(self):
        return self.dev(self.seq(1 - self.x, self.z, self.c), self.t)

    def quad(self, o):
        dx, dy = o // 2, o % 2
        x = (self.x + dx) % 2
        yb = (self.yb + dy) % 2
        return x, yb, self.dev(self.seq(x, self.z, self.c), self.t - self.yb + yb)

    def tens(self, o):
        t = (self.t + o) % 8
        return t, self.dev(self.s, t)

    def plane(self, o):
        j = (self.x * 8 + self.t + o) % 16
        x, t = j // 8, j % 8
        return j, self.dev(self.seq(x, self.z, self.c), t)


class Copies:
    def __init__(self, send, recv):
        self.send, self.recv, self.n, self.live = send, recv, 0, []

    def make(self, src, dst, dev):
        i = self.n
        self.n += 1
        assert i < self.send.shape[0]
        return pltpu.make_async_remote_copy(
            src_ref=src, dst_ref=dst, send_sem=self.send.at[i], recv_sem=self.recv.at[i],
            device_id=dev, device_id_type=MESH,
        )

    def go(self, src, dst, dev):
        cp = self.make(src, dst, dev)
        cp.start()
        self.live.append(cp)
        return cp

    def drain_sends(self):
        for cp in self.live:
            cp.wait_send()


def barrier(peers):
    sem = pltpu.get_barrier_semaphore()
    for dev in peers:
        pl.semaphore_signal(sem, inc=1, device_id=dev, device_id_type=MESH)
    pl.semaphore_wait(sem, len(peers))


def gather_grid(p, cps, own, view, nx, middle=lambda: None):
    size = (nx, 4)

    def send(h, a, b, sub, dim, sign):
        dx, dy = (a, b) if h == 0 else (b, a)
        dst = view(dx, dy, h, sub)
        return cps.go(own(h) if (a, b) == (0, 0) else dst, dst, p.near(dim, sign, nx))

    def spread(h, a, b, dim):
        return [send(h, a, b, None, dim, sign) for sign in ((1, -1) if size[dim] == 4 else (1,))]

    first = [spread(h, 0, 0, h) for h in range(2)]
    second = [{0: spread(h, 0, 0, 1 - h)} for h in range(2)]
    far = [[], []]
    last = []
    for i in range(2):
        for h in range(2):
            if i < len(first[h]):
                first[h][i].wait_recv()
                a = (-1, 1)[i]
                if size[h] == 4:
                    far[h].append(send(h, a, 0, i, h, -a))
                second[h][a] = spread(h, a, 0, 1 - h)

    def onward(h, a):
        for i, cp in enumerate(second[h][a]):
            cp.wait_recv()
            if size[1 - h] == 4:
                b = (-1, 1)[i]
                last.append(send(h, a, b, i, 1 - h, -b))

    for h in range(2):
        onward(h, 0)
    middle()
    for h in range(2):
        if far[h]:
            for cp in far[h]:
                cp.wait_recv()
            second[h][2] = spread(h, 2, 0, 1 - h)
    for a in (-1, 1, 2):
        for h in range(2):
            if a in second[h]:
                onward(h, a)
    for cp in last:
        cp.wait_recv()


ROW = (slice(0, 16), slice(16, 32))
COL = (slice(0, 1152), slice(1152, 2304))


def reduce_line(p, cps, read, view, buf, dim, nx):
    size = (nx, 4)[dim]
    rp, rm, up, dn, bu, bd = buf
    plus, minus = p.near(dim, 1, nx), p.near(dim, -1, nx)
    if size == 2:
        cp = cps.go(view(1, None), rp, plus)

        def finish():
            cp.wait_recv()
            return read(0, None) + rp[...].astype(f32)

        return [finish]
    far0 = cps.go(view(2, 0), up, plus)
    far1 = cps.go(view(2, 1), dn, minus)
    near = [cps.go(view(1, 1), rp.at[:, ROW[1]], plus), cps.go(view(-1, 0), rm.at[:, ROW[0]], minus)]

    def relay():
        far0.wait_recv()
        bu[...] = (read(1, 0) + up[...].astype(f32)).astype(bf16)
        near.append(cps.go(bu, rp.at[:, ROW[0]], plus))
        far1.wait_recv()
        bd[...] = (read(-1, 1) + dn[...].astype(f32)).astype(bf16)
        near.append(cps.go(bd, rm.at[:, ROW[1]], minus))

    def finish():
        for cp in near:
            cp.wait_recv()
        return read(0, None) + rp[...].astype(f32) + rm[...].astype(f32)

    return [relay, finish]


def reduce_grid(p, cps, part, bufs, sums, nx):
    at = (p.X if nx == 4 else p.X % 2, p.Y)
    size = (nx, 4)

    def one(h):
        def view(d, sub):
            rows = slice(0, 32) if sub is None else ROW[sub]
            i = (at[1 - h] + size[1 - h] + d) % size[1 - h]
            return part.at[:, i, rows, COL[h]] if h == 0 else part.at[i, :, rows, COL[h]]

        def read(d, sub):
            return view(d, sub)[...].astype(f32)

        return reduce_line(p, cps, read, view, bufs[h][:6], 1 - h, nx)

    def two(h):
        def view(d, sub):
            rows = slice(0, 32) if sub is None else ROW[sub]
            i = (at[h] + size[h] + d) % size[h]
            return sums[h].at[pl.ds(i, 1), rows]

        def read(d, sub):
            return view(d, sub)[...].astype(f32)

        return reduce_line(p, cps, read, view, bufs[h][6:], h, nx)

    steps = [one(h) for h in range(2)]
    for h in range(2):
        if len(steps[h]) == 2:
            steps[h][0]()
    later = []
    for h in range(2):
        sums[h][...] = steps[h][-1]().astype(bf16)
        later.append(two(h))
    for h in range(2):
        if len(later[h]) == 2:
            later[h][0]()
    return [later[h][-1]()[0] for h in range(2)]


def reduce_scratch(nx):
    out = []
    for h in range(2):
        size = (nx, 4)
        for n, m in ((size[h], size[1 - h]), (1, size[h])):
            del m
            out += [pltpu.VMEM((n, 32, 1152), bf16)] * 2 + [pltpu.VMEM((n, 16, 1152), bf16)] * 4
        out.append(pltpu.VMEM((size[h], 32, 1152), bf16))
    return out


def reduce_bufs(refs):
    return [refs[0:12], refs[13:25]], [refs[12], refs[25]]


def normed(values, gain):
    return values * lax.rsqrt(jnp.mean(values * values, axis=1, keepdims=True) + EPS) * gain[...][None, :]


def weight_send(p, cps, ws, own, d):
    org = p.x if own else 1 - p.x
    got = []
    for sign, dev in ((-1, p.zp()), (1, p.zm())):
        if d == 4 and (sign == -1) != own:
            continue
        slot = ((p.z + 8 + sign * (d - 1)) % 8) * 2 + p.c
        got += [(cps.go(w.at[org, slot], w.at[org, slot], dev), w, sign) for w in ws]
    return org, got, d


def weight_take(p, cps, sent):
    org, got, d = sent
    out = []
    for cp, w, sign in got:
        cp.wait_recv()
        slot = ((p.z + 8 + sign * d) % 8) * 2 + p.c
        out.append(cps.go(w.at[org, slot], w.at[org, slot], p.sib()))
    return out


def gather_hidden(ht, gate, up, down, xt, wg, wu, wd, send, recv, loc):
    p = Place()
    barrier(p.around(2) + [p.xpart(), p.zp(), p.zm(), p.sib()])
    cps = Copies(send, recv)
    ws = (wg, wu, wd)
    slot = p.z * 2 + p.c
    mine = pl.ds(pl.multiple_of(p.x * FFO, 128), FFP)
    other = pl.ds(pl.multiple_of((1 - p.x) * FFO, 128), FFP)
    swaps = [cps.go(a.at[:, other], w.at[p.x, slot], p.xpart()) for a, w in zip((gate, up, down), ws)]
    ring = [(cps.go(a.at[:, mine], w.at[p.x, slot], dev), w, sign)
            for sign, dev in ((-1, p.zp()), (1, p.zm())) for a, w in zip((gate, up, down), ws)]
    locs = [pltpu.make_async_copy(a.at[:, mine], w.at[p.x, slot], loc.at[i])
            for i, (a, w) in enumerate(zip((gate, up, down), ws))]
    sib = [cps.go(a.at[:, mine], w.at[p.x, slot], p.sib()) for a, w in zip((gate, up, down), ws)]

    def view(dx, dy, h, sub):
        t = ((p.t // 4 + 2 + dx) % 2) * 4 + (p.Y + 4 + dy) % 4
        low, n = ((0, 144) if sub is None else ((0, 80), (80, 64))[sub])
        return xt.at[t, pl.ds(h * 144 + low, n)]

    locs.append(pltpu.make_async_copy(ht, xt.at[p.t], loc.at[3]))
    for cp in locs:
        cp.start()
    swapped = []

    def middle():
        for cp in swaps:
            cp.wait_recv()
        swapped.append(weight_send(p, cps, ws, False, 1))
        for w in ws:
            sib.append(cps.go(w.at[1 - p.x, slot], w.at[1 - p.x, slot], p.sib()))
        sib.extend(weight_take(p, cps, (p.x, ring, 1)))

    gather_grid(p, cps, lambda h: ht.at[pl.ds(h * 144, 144)], view, 2, middle)
    sib += weight_take(p, cps, swapped[0])
    for cp in locs:
        cp.wait()
    for cp in sib:
        cp.wait_recv()
    cps.drain_sends()


def exchange_kv(stay, go, q, kv, qa, send, recv, loc):
    p = Place()
    quads = [p.quad(o) for o in range(1, 4)]
    barrier([d for _, _, d in quads] + [p.zp(), p.zm(), p.sib()])
    cps = Copies(send, recv)
    slot = p.z * 2 + p.c
    parts = (p.yb, 1 - p.yb)
    pair = cps.go(go, kv.at[p.yb, slot], quads[0][2])
    got = [[cps.go(stay, kv.at[p.yb, slot], p.zp()), cps.go(stay, kv.at[p.yb, slot], p.zm())]]
    locs = [pltpu.make_async_copy(stay, kv.at[p.yb, slot], loc.at[0]),
            pltpu.make_async_copy(q, qa.at[p.x * 2 + p.yb], loc.at[1])]
    for cp in locs:
        cp.start()
    sib = [cps.go(stay, kv.at[p.yb, slot], p.sib())]
    qs = [cps.go(q, qa.at[p.x * 2 + p.yb], d) for _, _, d in quads]
    pair.wait_recv()
    own = kv.at[1 - p.yb, slot]
    got.append([cps.go(own, own, p.zp()), cps.go(own, own, p.zm())])
    sib.append(cps.go(own, own, p.sib()))
    for d in range(1, 5):
        right = ((p.z + 8 - d) % 8) * 2 + p.c
        left = ((p.z + d) % 8) * 2 + p.c
        nxt = [[], []]
        for i, part in enumerate(parts):
            for side, cp in enumerate(got[i]):
                cp.wait_recv()
                if d < 4:
                    here = kv.at[part, (right, left)[side]]
                    if d < 3 or side == i:
                        nxt[i].append(cps.go(here, here, (p.zp(), p.zm())[side]))
                    sib.append(cps.go(here, here, p.sib()))
                else:
                    here = kv.at[part, right]
                    sib.append(cps.go(here, here, p.sib()))
        got = nxt
    for cp in locs:
        cp.wait()
    for cp in qs + sib:
        cp.wait_recv()
    cps.drain_sends()


def exchange_partials(num, den, wg0, wu0, wd0, rn, rd, wg, wu, wd, send, recv):
    p = Place()
    quads = [p.quad(o)[2] for o in range(1, 4)]
    barrier(quads + [p.zp(), p.zm(), p.sib()])
    cps = Copies(send, recv)
    ex = [cps.go(num.at[o + 1], rn.at[o], d) for o, d in enumerate(quads)]
    ex += [cps.go(den.at[o + 1], rd.at[o], d) for o, d in enumerate(quads)]
    sib = weight_take(p, cps, weight_send(p, cps, (wg, wu, wd), True, 2))
    for cp in ex + sib:
        cp.wait_recv()
    cps.drain_sends()


def mix_tensor(o_ref, hid, post_gain, ff_gain, wg0, wu0, wd0, mid, xa, wg, wu, wd, send, recv, loc, mine, *scratch):
    p = Place()
    barrier(p.around(4) + [p.zp(), p.zm(), p.sib()])
    cps = Copies(send, recv)
    ws = (wg, wu, wd)
    rest = [weight_send(p, cps, ws, False, 2), weight_send(p, cps, ws, True, 3)]
    bufs, sums = reduce_bufs(scratch)
    total = jnp.concatenate(reduce_grid(p, cps, o_ref, bufs, sums, 2), axis=1)
    middle = (hid[...].astype(f32) + normed(total, post_gain)).astype(bf16)
    mid[...] = middle
    mine[...] = normed(middle.astype(f32), ff_gain).astype(bf16)
    lc = pltpu.make_async_copy(mine, xa.at[p.X, p.Y], loc.at[0])
    lc.start()
    sib = weight_take(p, cps, rest[0])
    rest.append(weight_send(p, cps, ws, False, 3))
    sib += weight_take(p, cps, rest[1])
    rest.append(weight_send(p, cps, ws, True, 4))

    def middle_step():
        sib.extend(weight_take(p, cps, rest[2]))
        rest.append(weight_send(p, cps, ws, False, 4))

    def view(dx, dy, h, sub):
        rows = slice(0, 32) if sub is None else ROW[sub]
        return xa.at[(p.X + 4 + dx) % 4, (p.Y + 4 + dy) % 4, rows, COL[h]]

    gather_grid(p, cps, lambda h: mine.at[:, COL[h]], view, 4, middle_step)
    sib += weight_take(p, cps, rest[3])
    sib += weight_take(p, cps, rest[4])
    for cp in sib:
        cp.wait_recv()
    lc.wait()
    cps.drain_sends()


def mix_plane(y_ref, mid, gain, xa, send, recv, loc, mine, *scratch):
    p = Place()
    barrier(p.around(4))
    cps = Copies(send, recv)
    bufs, sums = reduce_bufs(scratch)
    total = jnp.concatenate(reduce_grid(p, cps, y_ref, bufs, sums, 4), axis=1)
    mine[...] = (mid[...].astype(f32) + normed(total, gain)).astype(bf16)
    lc = pltpu.make_async_copy(mine, xa.at[p.t], loc.at[0])
    lc.start()

    def view(dx, dy, h, sub):
        rows = slice(0, 32) if sub is None else ROW[sub]
        return xa.at[((p.X + 2 + dx) % 2) * 4 + (p.Y + 4 + dy) % 4, rows, COL[h]]

    gather_grid(p, cps, lambda h: mine.at[:, COL[h]], view, 2)
    lc.wait()
    cps.drain_sends()


def call(body, cid, ins, in_specs, outs, out_specs, n, n_loc=0, aliases=None, extra=()):
    scratch = [pltpu.SemaphoreType.DMA((n,)), pltpu.SemaphoreType.DMA((n,))]
    if n_loc:
        scratch.append(pltpu.SemaphoreType.DMA((n_loc,)))
    return pl.pallas_call(
        body,
        out_shape=[s if isinstance(s, jax.ShapeDtypeStruct) else jax.ShapeDtypeStruct(s, bf16) for s in outs],
        in_specs=in_specs,
        out_specs=out_specs,
        scratch_shapes=scratch + list(extra),
        input_output_aliases=aliases or {},
        compiler_params=pltpu.CompilerParams(collective_id=cid, has_side_effects=True),
        name=body.__name__,
    )(*ins)


def attend(lengths, owner, table, qa, kv, out, out_den, out_page, acc, den):
    p = Place()
    e0 = lengths[0]
    e1 = e0 + lengths[1]
    e2 = e1 + lengths[2]

    def start_of(tag):
        return jnp.where(tag >= e2, e2, jnp.where(tag >= e1, e1, jnp.where(tag >= e0, e0, 0)))

    row = lax.broadcasted_iota(jnp.int32, (128, 128), 0)
    lane = lax.broadcasted_iota(jnp.int32, (128, 128), 1)

    def key_block(k):
        b = owner[p.x * 16 + k]
        return jnp.where((p.yb + k // 2) % 2 == 0, b, 63 - b)

    def rel(x, h):
        return ((x + p.x) % 2) * 2 + (h + p.yb) % 2

    for qb in range(4):
        x, blk = qb // 2, qb % 2
        rows = pl.ds(blk * 128, 128)
        acc[...] = jnp.zeros_like(acc)
        den[...] = jnp.zeros_like(den)
        b = owner[x * 16 + p.z * 2 + p.c]
        q_block = b if blk == 0 else 63 - b
        first = start_of(q_block * 128)

        def step(k, carry):
            k_block = key_block(k)

            @pl.when((k_block <= q_block) & (k_block * 128 + 127 >= first))
            def _():
                qt = jnp.concatenate([qa[2 * x, rows, :], qa[2 * x + 1, rows, :]], axis=0)
                score = lax.dot_general(qt, kv[0, k], (((1,), (1,)), ((), ())), preferred_element_type=f32)
                capped = SOFT_CAP * jnp.tanh(score * (0.0625 / SOFT_CAP))
                tag = q_block * 128 + row
                kt = k_block * 128 + lane
                ok = (kt <= tag) & (kt >= start_of(tag))
                weight = jnp.exp(capped)
                weight = jnp.concatenate(
                    [jnp.where(ok, weight[:128], 0.0), jnp.where(ok, weight[128:], 0.0)], axis=0
                ).astype(bf16)
                den[...] += weight.astype(f32)
                acc[...] += jnp.dot(weight, kv[1, k], preferred_element_type=f32)
            return carry

        lax.fori_loop(0, 16, step, 0)
        total = lax.dot_general(
            jnp.ones((8, 128), f32), den[...], (((1,), (1,)), ((), ())),
            precision=lax.Precision.HIGHEST, preferred_element_type=f32,
        )
        num = acc[...].astype(bf16)
        for h in range(2):
            out[rel(x, h), rows, :] = num[h * 128:(h + 1) * 128]
            out_den[rel(x, h), :, blk * 128:(blk + 1) * 128] = total[:, h * 128:(h + 1) * 128]

    base = p.z * 4 + p.c * 2

    def look(i, found):
        page = table[i]
        return tuple(jnp.where(page == (n // 2) * 32 + base + n % 2, i, f) for n, f in enumerate(found))

    wanted = lax.fori_loop(0, 64, look, (jnp.int32(0),) * 4)

    def match(k, found):
        block = key_block(k)
        return tuple(jnp.where(block == w, k, f) for w, f in zip(wanted, found))

    chosen = lax.fori_loop(0, 16, match, (jnp.int32(-1),) * 4)
    for n in range(4):
        at = jnp.maximum(chosen[n], 0)
        for part in range(2):
            picked = jnp.where(chosen[n] >= 0, kv[part, at].astype(f32), 0.0)
            out_page[rel(n // 2, part), pl.ds((n % 2) * 128, 128), :] = picked.astype(bf16)


def project(normal, wq_ref, wk_ref, cosine, sine, yb):
    dims = (((1,), (0,)), ((), ()))
    q = lax.dot_general(normal, wq_ref[...], dims, preferred_element_type=f32)
    k = lax.dot_general(normal, wk_ref[...], dims, preferred_element_type=f32)
    c, s = cosine[...], sine[...]
    key = yb == 0

    def spin(v, turn):
        a, b = v[:, :128], v[:, 128:]
        both = jnp.concatenate([a * c - b * s, b * c + a * s], axis=1)
        return both if turn is None else jnp.where(turn, both, v)

    return spin(q, None).astype(bf16), spin(k, key).astype(bf16)


def first_layer(xt, gain, wq, wk, cosine, sine, stay, go, q_ref):
    p = Place()
    rows = jnp.transpose(xt[...].reshape(2304, 256).astype(f32))
    q, own = project(normed(rows, gain).astype(bf16), wq, wk, cosine, sine, p.yb)
    q_ref[...] = q
    low = (p.yb + p.z) % 2 == 0
    stay[...] = jnp.where(low, own[:128].astype(f32), own[128:].astype(f32)).astype(bf16)
    go[...] = jnp.where(low, own[128:].astype(f32), own[:128].astype(f32)).astype(bf16)


def next_layer(fr, gain, wq, wk, cosine, sine, ho, q_ref, k_ref):
    p = Place()
    rows = fr[...].reshape(256, 2304).astype(f32)
    q_ref[...], k_ref[...] = project(normed(rows, gain).astype(bf16), wq, wk, cosine, sine, p.yb)
    begin = p.t * 288
    tile = pl.multiple_of((begin // 128) * 128, 128)
    for i in range(8):
        window = fr[i, :, pl.ds(tile, 384)].astype(f32)
        moved = pltpu.roll(window, (384 - begin % 128) % 384, 1)
        ho[i * 32:(i + 1) * 32, :] = moved[:, :288].astype(bf16)


def feed_forward(xa, wg, wu, wd, out, vg, vu, vd, sem):
    p = Place()
    cps = [pltpu.make_async_copy(w, v, sem.at[i]) for i, (w, v) in enumerate(((wg, vg), (wu, vu), (wd, vd)))]
    for cp in cps:
        cp.start()
    cps[0].wait()
    cps[1].wait()
    lane = lax.broadcasted_iota(jnp.int32, (128, FFP), 1)
    keep = (lane >= FFP - FFO) | (p.x == 0)
    dims = (((1,), (1,)), ((), ()))
    for i in range(4):
        if i == 1:
            cps[2].wait()
        x = xa[i].reshape(128, 2304)
        g = jnp.dot(x, vg[...], preferred_element_type=f32)
        u = jnp.dot(x, vu[...], preferred_element_type=f32)
        inner = jnp.where(keep, jax.nn.gelu(g, approximate=True) * u, 0.0).astype(bf16)
        if i == 0:
            held = inner
            continue
        if i == 1:
            out[0] = lax.dot_general(held, vd[...], dims, preferred_element_type=f32).astype(bf16).reshape(4, 32, 2304)
        out[i] = lax.dot_general(inner, vd[...], dims, preferred_element_type=f32).astype(bf16).reshape(4, 32, 2304)


def local_call(body, ins, in_specs, outs, scratch=()):
    return pl.pallas_call(
        body,
        out_shape=[jax.ShapeDtypeStruct(s, bf16) for s in outs],
        in_specs=in_specs,
        out_specs=[VM] * len(outs),
        scratch_shapes=list(scratch),
        name=body.__name__,
    )(*ins)


def quad_route(dx, dy):
    route = []
    for s in range(32):
        for t in range(8):
            route.append((s * 8 + t, ((s + 16 * dx) % 32) * 8 + (t ^ dy)))
    return route


def starts_of(tags, lengths):
    e0 = lengths[0]
    e1 = e0 + lengths[1]
    e2 = e1 + lengths[2]
    return jnp.where(tags >= e2, e2, jnp.where(tags >= e1, e1, jnp.where(tags >= e0, e0, 0)))


def body(
    hidden, attn_gain, query_weight, kv_weight, out_weight, post_gain, ff_gain, ff_post_gain,
    gate_weight, up_weight, down_weight_t, next_gain, next_query_weight, next_kv_weight,
    lengths, pair_owner, page_table,
):
    p = Place()
    is_key = p.yb == 0
    owned = jnp.sum(jnp.where(jnp.arange(32, dtype=jnp.int32) == p.s, pair_owner, 0))
    local = jnp.arange(256, dtype=jnp.int32)
    tags = jnp.where(local < 128, owned * 128 + local, (63 - owned) * 128 + local - 128)
    position = tags - starts_of(tags, lengths)
    freq_vec = 10000.0 ** (-jnp.arange(128, dtype=f32) / 128)
    angles = position.astype(f32)[:, None] * freq_vec[None, :]
    cosine, sine = jnp.cos(angles), jnp.sin(angles)

    wshape = (2, 16, 72, FFP)
    xt, wg, wu, wd = call(
        gather_hidden, 1, (hidden.T, gate_weight, up_weight, down_weight_t), [VM] * 4,
        [(8, 288, 256), wshape, wshape, wshape], [VM, AN, AN, AN], 64, 4,
    )
    stay, go, queries = local_call(
        first_layer, (xt, attn_gain, query_weight, kv_weight, cosine, sine), [VM] * 6,
        [(128, 256), (128, 256), (256, 256)],
    )
    kv, qa = call(
        exchange_kv, 2, (stay, go, queries), [VM] * 3, [(2, 16, 128, 256), (4, 256, 256)], [VM, VM], 40, 2,
    )
    num, den, page = pl.pallas_call(
        attend,
        out_shape=[jax.ShapeDtypeStruct((4, 256, 256), bf16), jax.ShapeDtypeStruct((4, 8, 256), f32),
                   jax.ShapeDtypeStruct((4, 256, 256), bf16)],
        in_specs=[pl.BlockSpec(memory_space=pltpu.SMEM)] * 3 + [VM] * 2,
        out_specs=[VM] * 3,
        scratch_shapes=[pltpu.VMEM((256, 256), f32), pltpu.VMEM((256, 128), f32)],
        name="attend",
    )(lengths, pair_owner, page_table, qa, kv)
    rn, rd, wg, wu, wd = call(
        exchange_partials, 3, (num, den, wg, wu, wd), [VM, VM, AN, AN, AN],
        [(3, 256, 256), jax.ShapeDtypeStruct((3, 8, 256), f32), wshape, wshape, wshape],
        [VM, VM, AN, AN, AN], 20, 0, {2: 2, 3: 3, 4: 4},
    )
    pages = page[0].astype(f32)
    for o in range(1, 4):
        pages += lax.ppermute(page[o], ("seq", "tensor"), quad_route(o // 2, o % 2)).astype(f32)
    kv_pages = pages.astype(bf16).reshape(2, 128, 256)
    numerator = num[0].astype(f32) + rn[0].astype(f32) + rn[1].astype(f32) + rn[2].astype(f32)
    denominator = (den[0] + rd[0] + rd[1] + rd[2])[0][:, None]
    attended = (numerator / denominator).astype(bf16)
    partial = jnp.dot(attended, out_weight, preferred_element_type=f32).astype(bf16).reshape(2, 4, 32, 2304)
    own_hidden = lax.dynamic_slice_in_dim(xt.reshape(2304, 256), p.t * 32, 32, 1).T
    mine = pltpu.VMEM((32, 2304), bf16)
    middle, xa, wg, wu, wd = call(
        mix_tensor, 4, (partial, own_hidden, post_gain, ff_gain, wg, wu, wd), [VM] * 4 + [AN] * 3,
        [(32, 2304), (4, 4, 32, 2304), wshape, wshape, wshape], [VM, VM, AN, AN, AN], 104, 1,
        {4: 2, 5: 3, 6: 4}, [mine] + reduce_scratch(2),
    )
    (ff_partial,) = local_call(
        feed_forward, (xa, wg.reshape(2304, FFP), wu.reshape(2304, FFP), wd.reshape(2304, FFP)), [VM] + [AN] * 3,
        [(4, 4, 32, 2304)], [pltpu.VMEM((2304, FFP), bf16)] * 3 + [pltpu.SemaphoreType.DMA((3,))],
    )
    (fr,) = call(
        mix_plane, 5, (ff_partial, middle, ff_post_gain), [VM] * 3, [(8, 32, 2304)], [VM], 60, 1, None,
        [mine] + reduce_scratch(4),
    )
    hidden_out, next_query, next_kv = local_call(
        next_layer, (fr, next_gain, next_query_weight, next_kv_weight, cosine, sine), [VM] * 6,
        [(256, 288), (256, 256), (256, 256)],
    )
    return (hidden_out, next_query, next_kv, kv_pages)


def solution(mesh):
    wide = P("seq", "tensor")
    cols = P(None, "tensor")
    in_specs = (wide, P(), cols, cols, P("tensor", None), P(), P(), P(), wide, wide, wide, P(), cols, cols, P(), P(), P())
    out_specs = (wide, wide, wide, P("seq", None, "tensor"))
    return jax.shard_map(body, mesh=mesh, in_specs=in_specs, out_specs=out_specs, check_vma=False)
```

```python
import jax
import jax.numpy as jnp
from jax import lax
from jax.experimental import pallas as pl
from jax.experimental.pallas import tpu as pltpu
import numpy as np
from jax.sharding import PartitionSpec as P

EPS = 1e-06
SOFT_CAP = 50.0
MESH = pl.DeviceIdType.MESH
VM = pl.BlockSpec(memory_space=pltpu.VMEM)
AN = pl.BlockSpec(memory_space=pl.ANY)
FFP = 640
FFO = 512
bf16 = jnp.bfloat16
f32 = jnp.float32


class Place:
    def __init__(self):
        self.s = lax.axis_index("seq")
        self.t = lax.axis_index("tensor")
        self.x = self.s // 16
        self.z = (self.s // 2) % 8
        self.c = self.s % 2
        self.yb = self.t % 2
        self.X = self.x * 2 + self.t // 4
        self.Y = self.t % 4

    def grid(self, X, Y):
        return self.dev(self.seq(X // 2, self.z, self.c), (X % 2) * 4 + Y)

    def near(self, dim, sign, nx):
        if dim == 1:
            return self.grid(self.X, (self.Y + 4 + sign) % 4)
        if nx == 2:
            return self.dev(self.s, (self.t + 4) % 8)
        return self.grid((self.X + 4 + sign) % 4, self.Y)

    def around(self, nx):
        out = [self.near(1, 1, nx), self.near(1, -1, nx), self.near(0, 1, nx)]
        return out + ([self.near(0, -1, nx)] if nx == 4 else [])

    def seq(self, x, z, c):
        return x * 16 + z * 2 + c

    def dev(self, s, t):
        return {"seq": s, "tensor": t}

    def zp(self):
        return self.dev(self.seq(self.x, (self.z + 1) % 8, self.c), self.t)

    def zm(self):
        return self.dev(self.seq(self.x, (self.z + 7) % 8, self.c), self.t)

    def sib(self):
        return self.dev(self.seq(self.x, self.z, 1 - self.c), self.t)

    def xpart(self):
        return self.dev(self.seq(1 - self.x, self.z, self.c), self.t)

    def quad(self, o):
        dx, dy = o // 2, o % 2
        x = (self.x + dx) % 2
        yb = (self.yb + dy) % 2
        return x, yb, self.dev(self.seq(x, self.z, self.c), self.t - self.yb + yb)

    def tens(self, o):
        t = (self.t + o) % 8
        return t, self.dev(self.s, t)

    def plane(self, o):
        j = (self.x * 8 + self.t + o) % 16
        x, t = j // 8, j % 8
        return j, self.dev(self.seq(x, self.z, self.c), t)


class Copies:
    def __init__(self, send, recv):
        self.send, self.recv, self.n, self.live = send, recv, 0, []

    def make(self, src, dst, dev):
        i = self.n
        self.n += 1
        assert i < self.send.shape[0]
        return pltpu.make_async_remote_copy(
            src_ref=src, dst_ref=dst, send_sem=self.send.at[i], recv_sem=self.recv.at[i],
            device_id=dev, device_id_type=MESH,
        )

    def go(self, src, dst, dev):
        cp = self.make(src, dst, dev)
        cp.start()
        self.live.append(cp)
        return cp

    def drain_sends(self):
        for cp in self.live:
            cp.wait_send()


def barrier(peers):
    sem = pltpu.get_barrier_semaphore()
    for dev in peers:
        pl.semaphore_signal(sem, inc=1, device_id=dev, device_id_type=MESH)
    pl.semaphore_wait(sem, len(peers))


def gather_grid(p, cps, own, view, nx, middle=lambda: None):
    size = (nx, 4)

    def send(h, a, b, sub, dim, sign):
        dx, dy = (a, b) if h == 0 else (b, a)
        dst = view(dx, dy, h, sub)
        return cps.go(own(h) if (a, b) == (0, 0) else dst, dst, p.near(dim, sign, nx))

    def spread(h, a, b, dim):
        return [send(h, a, b, None, dim, sign) for sign in ((1, -1) if size[dim] == 4 else (1,))]

    first = [spread(h, 0, 0, h) for h in range(2)]
    second = [{0: spread(h, 0, 0, 1 - h)} for h in range(2)]
    far = [[], []]
    last = []
    for i in range(2):
        for h in range(2):
            if i < len(first[h]):
                first[h][i].wait_recv()
                a = (-1, 1)[i]
                if size[h] == 4:
                    far[h].append(send(h, a, 0, i, h, -a))
                second[h][a] = spread(h, a, 0, 1 - h)

    def onward(h, a):
        for i, cp in enumerate(second[h][a]):
            cp.wait_recv()
            if size[1 - h] == 4:
                b = (-1, 1)[i]
                last.append(send(h, a, b, i, 1 - h, -b))

    for h in range(2):
        onward(h, 0)
    middle()
    for h in range(2):
        if far[h]:
            for cp in far[h]:
                cp.wait_recv()
            second[h][2] = spread(h, 2, 0, 1 - h)
    for a in (-1, 1, 2):
        for h in range(2):
            if a in second[h]:
                onward(h, a)
    for cp in last:
        cp.wait_recv()


ROW = (slice(0, 16), slice(16, 32))
COL = (slice(0, 1152), slice(1152, 2304))


def reduce_line(p, cps, read, view, buf, dim, nx):
    size = (nx, 4)[dim]
    rp, rm, up, dn, bu, bd = buf
    plus, minus = p.near(dim, 1, nx), p.near(dim, -1, nx)
    if size == 2:
        cp = cps.go(view(1, None), rp, plus)

        def finish():
            cp.wait_recv()
            return read(0, None) + rp[...].astype(f32)

        return [finish]
    far0 = cps.go(view(2, 0), up, plus)
    far1 = cps.go(view(2, 1), dn, minus)
    near = [cps.go(view(1, 1), rp.at[:, ROW[1]], plus), cps.go(view(-1, 0), rm.at[:, ROW[0]], minus)]

    def relay():
        far0.wait_recv()
        bu[...] = (read(1, 0) + up[...].astype(f32)).astype(bf16)
        near.append(cps.go(bu, rp.at[:, ROW[0]], plus))
        far1.wait_recv()
        bd[...] = (read(-1, 1) + dn[...].astype(f32)).astype(bf16)
        near.append(cps.go(bd, rm.at[:, ROW[1]], minus))

    def finish():
        for cp in near:
            cp.wait_recv()
        return read(0, None) + rp[...].astype(f32) + rm[...].astype(f32)

    return [relay, finish]


def reduce_grid(p, cps, part, bufs, sums, nx):
    at = (p.X if nx == 4 else p.X % 2, p.Y)
    size = (nx, 4)

    def one(h):
        def view(d, sub):
            rows = slice(0, 32) if sub is None else ROW[sub]
            i = (at[1 - h] + size[1 - h] + d) % size[1 - h]
            return part.at[:, i, rows, COL[h]] if h == 0 else part.at[i, :, rows, COL[h]]

        def read(d, sub):
            return view(d, sub)[...].astype(f32)

        return reduce_line(p, cps, read, view, bufs[h][:6], 1 - h, nx)

    def two(h):
        def view(d, sub):
            rows = slice(0, 32) if sub is None else ROW[sub]
            i = (at[h] + size[h] + d) % size[h]
            return sums[h].at[pl.ds(i, 1), rows]

        def read(d, sub):
            return view(d, sub)[...].astype(f32)

        return reduce_line(p, cps, read, view, bufs[h][6:], h, nx)

    steps = [one(h) for h in range(2)]
    for h in range(2):
        if len(steps[h]) == 2:
            steps[h][0]()
    later = []
    for h in range(2):
        sums[h][...] = steps[h][-1]().astype(bf16)
        later.append(two(h))
    for h in range(2):
        if len(later[h]) == 2:
            later[h][0]()
    return [later[h][-1]()[0] for h in range(2)]


def reduce_scratch(nx):
    out = []
    for h in range(2):
        size = (nx, 4)
        for n, m in ((size[h], size[1 - h]), (1, size[h])):
            del m
            out += [pltpu.VMEM((n, 32, 1152), bf16)] * 2 + [pltpu.VMEM((n, 16, 1152), bf16)] * 4
        out.append(pltpu.VMEM((size[h], 32, 1152), bf16))
    return out


def reduce_bufs(refs):
    return [refs[0:12], refs[13:25]], [refs[12], refs[25]]


def normed(values, gain):
    return values * lax.rsqrt(jnp.mean(values * values, axis=1, keepdims=True) + EPS) * gain[...][None, :]


def weight_send(p, cps, ws, own, d):
    org = p.x if own else 1 - p.x
    got = []
    for sign, dev in ((-1, p.zp()), (1, p.zm())):
        if d == 4 and (sign == -1) != own:
            continue
        slot = ((p.z + 8 + sign * (d - 1)) % 8) * 2 + p.c
        got += [(cps.go(w.at[org, slot], w.at[org, slot], dev), w, sign) for w in ws]
    return org, got, d


def weight_take(p, cps, sent):
    org, got, d = sent
    out = []
    for cp, w, sign in got:
        cp.wait_recv()
        slot = ((p.z + 8 + sign * d) % 8) * 2 + p.c
        out.append(cps.go(w.at[org, slot], w.at[org, slot], p.sib()))
    return out


FREQ = (10000.0 ** (-np.arange(128, dtype=np.float64) / 128)).astype(np.float32)[None, :]


def starts_of(tags, e0, e1, e2):
    return jnp.where(tags >= e2, e2, jnp.where(tags >= e1, e1, jnp.where(tags >= e0, e0, 0)))


def attention_part(
    lengths, owner, table, ht, gate, up, down, freq, attn_gain, wq, wk, wo, post_gain, ff_gain,
    mid, xa, wg, wu, wd, page_out, cosine, sine,
    send, recv, loc, xt, rows_ref, stay, go, q_ref, kv, qa, start_ref, acc, den, num, dn, pg, rn, rd, rp, part, mine,
    *scratch,
):
    p = Place()
    quads = [p.quad(o) for o in range(1, 4)]
    barrier(p.around(4) + [d for _, _, d in quads[1:]] + [p.zp(), p.zm(), p.sib()])
    cps = Copies(send, recv)
    ws = (wg, wu, wd)
    slot = p.z * 2 + p.c

    columns = pl.ds(pl.multiple_of(p.x * FFO, 128), FFP)
    other = pl.ds(pl.multiple_of((1 - p.x) * FFO, 128), FFP)
    swaps = [cps.go(a.at[:, other], w.at[p.x, slot], p.xpart()) for a, w in zip((gate, up, down), ws)]
    ring = [(cps.go(a.at[:, columns], w.at[p.x, slot], dev), w, sign)
            for sign, dev in ((-1, p.zp()), (1, p.zm())) for a, w in zip((gate, up, down), ws)]
    locs = [pltpu.make_async_copy(a.at[:, columns], w.at[p.x, slot], loc.at[i])
            for i, (a, w) in enumerate(zip((gate, up, down), ws))]
    locs.append(pltpu.make_async_copy(ht, xt.at[p.t], loc.at[3]))
    sib = [cps.go(a.at[:, columns], w.at[p.x, slot], p.sib()) for a, w in zip((gate, up, down), ws)]
    for cp in locs:
        cp.start()

    e0 = lengths[0]
    e1 = e0 + lengths[1]
    e2 = e1 + lengths[2]
    row = lax.broadcasted_iota(jnp.int32, (128, 128), 0)
    lane = lax.broadcasted_iota(jnp.int32, (128, 128), 1)
    mypair = owner[p.s]
    for blk in range(2):
        tag = (mypair if blk == 0 else 63 - mypair) * 128 + row
        angle = (tag - starts_of(tag, e0, e1, e2)).astype(f32) * freq[...]
        cosine[blk * 128:(blk + 1) * 128, :] = jnp.cos(angle)
        sine[blk * 128:(blk + 1) * 128, :] = jnp.sin(angle)
    q_blocks = []
    for x in range(2):
        b = owner[x * 16 + p.z * 2 + p.c]
        q_blocks += [b, 63 - b]
    for n in range(4):
        start = starts_of(q_blocks[n] * 128 + row, e0, e1, e2)
        start_ref[n, 0:128, :] = start
        start_ref[n, 128:256, :] = start

    def view_hidden(dx, dy, h, sub):
        t = ((p.t // 4 + 2 + dx) % 2) * 4 + (p.Y + 4 + dy) % 4
        low, n = ((0, 144) if sub is None else ((0, 80), (80, 64))[sub])
        return xt.at[t, pl.ds(h * 144 + low, n)]

    swapped = []

    def middle():
        for cp in swaps:
            cp.wait_recv()
        swapped.append(weight_send(p, cps, ws, False, 1))
        for w in ws:
            sib.append(cps.go(w.at[1 - p.x, slot], w.at[1 - p.x, slot], p.sib()))

    gather_grid(p, cps, lambda h: ht.at[pl.ds(h * 144, 144)], view_hidden, 2, middle)
    locs[3].wait()

    rows = jnp.transpose(xt[...].reshape(2304, 256).astype(f32))
    rows_ref[...] = rows.astype(bf16).reshape(8, 32, 2304)
    normal = normed(rows, attn_gain).astype(bf16)
    own = turned(jnp.dot(normal, wk[...], preferred_element_type=f32), cosine, sine, p.yb == 0)
    low = (p.yb + p.z) % 2 == 0
    stay[...] = jnp.where(low, own[:128], own[128:]).astype(bf16)
    go[...] = jnp.where(low, own[128:], own[:128]).astype(bf16)
    ends = ((7, p.zp()), (1, p.zm()), (0, p.sib()))
    pair = cps.go(go, kv.at[p.yb, 0, p.c], quads[0][2])
    first = [cps.go(stay, kv.at[p.yb, r, p.c], dev) for r, dev in ends]
    got, shared = [first[:2]], [first[2:]]
    lq = [pltpu.make_async_copy(stay, kv.at[p.yb, 0, p.c], loc.at[4])]
    lq[0].start()
    query = turned(jnp.dot(normal, wq[...], preferred_element_type=f32), cosine, sine, None)
    q_ref[...] = query.astype(bf16).reshape(2, 128, 256)
    lq.append(pltpu.make_async_copy(q_ref, qa.at[p.x, p.yb], loc.at[5]))
    lq[1].start()
    pair.wait_recv()
    mate = kv.at[1 - p.yb, 0, p.c]
    first = [cps.go(mate, kv.at[1 - p.yb, r, p.c], dev) for r, dev in ends]
    got.append(first[:2])
    shared[0] += first[2:]
    qs = [cps.go(q_ref, qa.at[p.x, p.yb], d) for _, _, d in quads]
    acc[...] = jnp.zeros_like(acc)
    den[...] = jnp.zeros_like(den)
    for cp in lq:
        cp.wait()
    for cp in qs:
        cp.wait_recv()

    def key_block(z, c):
        b = owner[p.x * 16 + z * 2 + c]
        return jnp.where((p.yb + z) % 2 == 0, b, 63 - b)

    def attend(rel):
        z = (p.z + rel) % 8
        blocks = [key_block(z, c) for c in range(2)]
        keys = kv[0, rel].reshape(256, 256)
        values = kv[1, rel].reshape(256, 256)

        def tile(n, carry):
            b = owner[(n // 2) * 16 + p.z * 2 + p.c]
            q_block = jnp.where(n % 2 == 0, b, 63 - b)
            qt = jnp.concatenate([qa[n // 2, h, n % 2] for h in range(2)], axis=0)
            score = lax.dot_general(qt, keys, (((1,), (1,)), ((), ())), preferred_element_type=f32)
            weight = jnp.exp(SOFT_CAP * jnp.tanh(score * (0.0625 / SOFT_CAP)))
            start = start_ref[n]
            r = lax.broadcasted_iota(jnp.int32, (256, 128), 0) % 128
            l = lax.broadcasted_iota(jnp.int32, (256, 128), 1)
            rounded = []
            for c in range(2):
                kt = blocks[c] * 128 + l
                ok = (kt <= q_block * 128 + r) & (kt >= start)
                rounded.append(jnp.where(ok, weight[:, c * 128:(c + 1) * 128], 0.0).astype(bf16))
            den[n] += rounded[0].astype(f32) + rounded[1].astype(f32)
            acc[n] += jnp.dot(jnp.concatenate(rounded, axis=1), values, preferred_element_type=f32)
            return carry

        lax.fori_loop(0, 4, tile, 0)

    spots = [[0]]
    for d in range(1, 5):
        nxt = [[], []]
        now = []
        for i, kind in enumerate((p.yb, 1 - p.yb)):
            for side, cp in enumerate(got[i]):
                cp.wait_recv()
                rel = 8 - d if side == 0 else d
                here = kv.at[kind, rel, p.c]
                if d < 3 or (d == 3 and side == i):
                    further = kv.at[kind, rel - 1 if side == 0 else rel + 1, p.c]
                    nxt[i].append(cps.go(here, further, (p.zp(), p.zm())[side]))
                now.append(cps.go(here, here, p.sib()))
        got = nxt
        if d == 4:
            sib += weight_take(p, cps, (p.x, ring, 1))
            sib += weight_take(p, cps, swapped[0])
            rest = [weight_send(p, cps, ws, True, 2), weight_send(p, cps, ws, False, 2)]
        for cp in shared[d - 1]:
            cp.wait_recv()
        for rel in spots[d - 1]:
            attend(rel)
        shared.append(now)
        spots.append([8 - d, d] if d < 4 else [4])
    for cp in shared[4]:
        cp.wait_recv()
    attend(4)

    for n in range(4):
        below = lax.dot_general(
            jnp.ones((8, 128), f32), den[n], (((1,), (1,)), ((), ())),
            precision=lax.Precision.HIGHEST, preferred_element_type=f32,
        )
        for h in range(2):
            num[n // 2, h, n % 2] = acc[n, h * 128:(h + 1) * 128, :].astype(bf16)
            dn[n // 2, h, n % 2] = below[:, h * 128:(h + 1) * 128]
    ex = [cps.go(num.at[x, yb], rn.at[o], d) for o, (x, yb, d) in enumerate(quads)]
    ex += [cps.go(dn.at[x, yb], rd.at[o], d) for o, (x, yb, d) in enumerate(quads)]
    base = p.z * 4 + p.c * 2

    def look(i, found):
        page = table[i]
        return tuple(jnp.where(page == (n // 2) * 32 + base + n % 2, i, f) for n, f in enumerate(found))

    wanted = lax.fori_loop(0, 64, look, (jnp.int32(0),) * 4)

    def choose(n, carry):
        want = jnp.where(n == 0, wanted[0], jnp.where(n == 1, wanted[1], jnp.where(n == 2, wanted[2], wanted[3])))
        sums = [jnp.zeros((128, 256), f32)] * 2
        for rel in range(8):
            for c in range(2):
                take = jnp.where(key_block((p.z + rel) % 8, c) == want, 1.0, 0.0)
                sums = [a + kv[kind, rel, c].astype(f32) * take for kind, a in enumerate(sums)]
        for kind in range(2):
            pg[n // 2, kind, n % 2] = sums[kind].astype(bf16)
        return carry

    lax.fori_loop(0, 4, choose, 0)
    px = [cps.go(pg.at[x, yb], rp.at[o], d) for o, (x, yb, d) in enumerate(quads)]
    for cp in ex:
        cp.wait_recv()
    total = num[p.x, p.yb].astype(f32)
    below = dn[p.x, p.yb]
    for o in range(3):
        total += rn[o].astype(f32)
        below += rd[o]
    pieces = []
    for blk in range(2):
        inverse = jnp.transpose(jnp.broadcast_to(1.0 / below[blk, 0:1, :], (128, 128)))
        pieces.append((total[blk] * jnp.concatenate([inverse, inverse], axis=1)).astype(bf16))
    attended = jnp.concatenate(pieces, axis=0)
    part[...] = jnp.dot(attended, wo[...], preferred_element_type=f32).astype(bf16).reshape(2, 4, 32, 2304)
    sib += weight_take(p, cps, rest[0])
    sib += weight_take(p, cps, rest[1])
    rest = [weight_send(p, cps, ws, True, 3), weight_send(p, cps, ws, False, 3)]

    bufs, sums = reduce_bufs(scratch)
    total = jnp.concatenate(reduce_grid(p, cps, part, bufs, sums, 2), axis=1)
    middle_rows = (rows_ref[p.t].astype(f32) + normed(total, post_gain)).astype(bf16)
    mid[...] = middle_rows
    mine[...] = normed(middle_rows.astype(f32), ff_gain).astype(bf16)
    lc = pltpu.make_async_copy(mine, xa.at[p.X, p.Y], loc.at[6])
    lc.start()
    last = []

    def view(dx, dy, h, sub):
        rows = slice(0, 32) if sub is None else ROW[sub]
        return xa.at[(p.X + 4 + dx) % 4, (p.Y + 4 + dy) % 4, rows, COL[h]]

    def middle_step():
        sib.extend(weight_take(p, cps, rest[0]))
        last.append(weight_send(p, cps, ws, True, 4))
        sib.extend(weight_take(p, cps, rest[1]))
        last.append(weight_send(p, cps, ws, False, 4))

    gather_grid(p, cps, lambda h: mine.at[:, COL[h]], view, 4, middle_step)
    sib += weight_take(p, cps, last[0])
    sib += weight_take(p, cps, last[1])
    for cp in px:
        cp.wait_recv()
    pages = pg[p.x, p.yb].astype(f32)
    for o in range(3):
        pages += rp[o].astype(f32)
    page_out[...] = pages.astype(bf16)
    for cp in sib:
        cp.wait_recv()
    for cp in locs[:3] + [lc]:
        cp.wait()
    cps.drain_sends()


def turned(v, cosine, sine, turn):
    c, s = cosine[...], sine[...]
    if turn is not None:
        c = jnp.where(turn, c, 1.0)
        s = jnp.where(turn, s, 0.0)
    a, b = v[:, :128], v[:, 128:]
    return jnp.concatenate([a * c - b * s, b * c + a * s], axis=1)


def feed_part(xin, mid, gain, wg, wu, wd, xa, send, recv, loc, vgu, vd, inner, y_ref, mine, *scratch):
    p = Place()
    def fetch(j):
        cols = pl.ds(pl.multiple_of(j * 128, 128), 128)
        return [pltpu.make_async_copy(w.at[:, cols], vgu.at[:, pl.ds(pl.multiple_of(j * 256 + k * 128, 128), 128)], loc.at[2 * j + k])
                for k, w in enumerate((wg, wu))]

    for j in range(5):
        for cp in fetch(j):
            cp.start()
    lw = pltpu.make_async_copy(wd, vd, loc.at[10])
    lw.start()
    barrier(p.around(4))
    cps = Copies(send, recv)

    def block(j, carry):
        for cp in fetch(j):
            cp.wait()
        x = xin[...].reshape(512, 2304)
        both = jnp.dot(x, vgu[:, pl.ds(pl.multiple_of(j * 256, 256), 256)], preferred_element_type=f32)
        gate, up = both[:, :128], both[:, 128:]
        made = jax.nn.gelu(gate, approximate=True) * up
        keep = jnp.zeros(made.shape, jnp.int32) + (j + 1 - p.x) > 0
        inner[:, pl.ds(pl.multiple_of(j * 128, 128), 128)] = jnp.where(keep, made, 0.0).astype(bf16)
        return carry

    lax.fori_loop(0, 5, block, 0)
    lw.wait()

    def lower(n, carry):
        w = vd[pl.ds(pl.multiple_of(n * 256, 256), 256), :]
        out = lax.dot_general(inner[...], w, (((1,), (1,)), ((), ())), preferred_element_type=f32)
        y_ref[:, :, :, pl.ds(pl.multiple_of(n * 256, 256), 256)] = out.astype(bf16).reshape(4, 4, 32, 256)
        return carry

    lax.fori_loop(0, 9, lower, 0)
    bufs, sums = reduce_bufs(scratch)
    total = jnp.concatenate(reduce_grid(p, cps, y_ref, bufs, sums, 4), axis=1)
    mine[...] = (mid[...].astype(f32) + normed(total, gain)).astype(bf16)
    lc = pltpu.make_async_copy(mine, xa.at[p.t], loc.at[11])
    lc.start()

    def view(dx, dy, h, sub):
        rows = slice(0, 32) if sub is None else ROW[sub]
        return xa.at[((p.X + 2 + dx) % 2) * 4 + (p.Y + 4 + dy) % 4, rows, COL[h]]

    gather_grid(p, cps, lambda h: mine.at[:, COL[h]], view, 2)
    lc.wait()
    cps.drain_sends()


def call(body, cid, ins, in_specs, outs, out_specs, n, n_loc=0, aliases=None, extra=()):
    scratch = [pltpu.SemaphoreType.DMA((n,)), pltpu.SemaphoreType.DMA((n,))]
    if n_loc:
        scratch.append(pltpu.SemaphoreType.DMA((n_loc,)))
    return pl.pallas_call(
        body,
        out_shape=[s if isinstance(s, jax.ShapeDtypeStruct) else jax.ShapeDtypeStruct(s, bf16) for s in outs],
        in_specs=in_specs,
        out_specs=out_specs,
        scratch_shapes=scratch + list(extra),
        input_output_aliases=aliases or {},
        compiler_params=pltpu.CompilerParams(collective_id=cid, has_side_effects=True),
        name=body.__name__,
    )(*ins)


def next_layer(fr, gain, wq, wk, cosine, sine, page, ho, q_ref, k_ref, page_out):
    p = Place()
    rows = fr[...].reshape(256, 2304).astype(f32)
    normal = normed(rows, gain).astype(bf16)
    q_ref[...] = turned(jnp.dot(normal, wq[...], preferred_element_type=f32), cosine, sine, None).astype(bf16)
    k_ref[...] = turned(jnp.dot(normal, wk[...], preferred_element_type=f32), cosine, sine, p.yb == 0).astype(bf16)
    begin = p.t * 288
    tile = pl.multiple_of((begin // 128) * 128, 128)
    window = fr[:, :, pl.ds(tile, 384)].reshape(256, 384).astype(f32)
    moved = jnp.transpose(pltpu.roll(window, (384 - begin % 128) % 384, 1))
    ho[...] = moved[:288, :].astype(bf16)
    page_out[...] = page[...]


def local_call(body, ins, in_specs, outs, scratch=()):
    return pl.pallas_call(
        body,
        out_shape=[jax.ShapeDtypeStruct(s, bf16) for s in outs],
        in_specs=in_specs,
        out_specs=[VM] * len(outs),
        scratch_shapes=list(scratch),
        name=body.__name__,
    )(*ins)


def quad_route(dx, dy):
    route = []
    for s in range(32):
        for t in range(8):
            route.append((s * 8 + t, ((s + 16 * dx) % 32) * 8 + (t ^ dy)))
    return route


def body(
    hidden, attn_gain, query_weight, kv_weight, out_weight, post_gain, ff_gain, ff_post_gain,
    gate_weight, up_weight, down_weight_t, next_gain, next_query_weight, next_kv_weight,
    lengths, pair_owner, page_table,
):
    wshape = (2, 16, 72, FFP)
    vmem = pltpu.VMEM
    angle = jax.ShapeDtypeStruct((256, 128), f32)
    mine = vmem((32, 2304), bf16)
    middle, xa, wg, wu, wd, page, cosine, sine = call(
        attention_part, 1,
        (lengths, pair_owner, page_table, hidden.T, gate_weight, up_weight, down_weight_t, jnp.asarray(FREQ), attn_gain,
         query_weight, kv_weight, out_weight, post_gain, ff_gain),
        [pl.BlockSpec(memory_space=pltpu.SMEM)] * 3 + [VM] * 11,
        [(32, 2304), (4, 4, 32, 2304), wshape, wshape, wshape, (2, 128, 256), angle, angle],
        [VM, VM, AN, AN, AN, VM, VM, VM], 224, 7, None,
        [vmem((8, 288, 256), bf16), vmem((8, 32, 2304), bf16), vmem((128, 256), bf16), vmem((128, 256), bf16),
         vmem((2, 128, 256), bf16), vmem((2, 8, 2, 128, 256), bf16), vmem((2, 2, 2, 128, 256), bf16),
         vmem((4, 256, 128), jnp.int32), vmem((4, 256, 256), f32), vmem((4, 256, 128), f32),
         vmem((2, 2, 2, 128, 256), bf16), vmem((2, 2, 2, 8, 128), f32), vmem((2, 2, 2, 128, 256), bf16),
         vmem((3, 2, 128, 256), bf16), vmem((3, 2, 8, 128), f32), vmem((3, 2, 128, 256), bf16),
         vmem((2, 4, 32, 2304), bf16), mine] + reduce_scratch(2),
    )
    (fr,) = call(
        feed_part, 2,
        (xa, middle, ff_post_gain, wg.reshape(2304, FFP), wu.reshape(2304, FFP), wd.reshape(2304, FFP)), [VM] * 3 + [AN] * 3,
        [(8, 32, 2304)], [VM], 60, 12, None,
        [vmem((2304, 2 * FFP), bf16), vmem((2304, FFP), bf16), vmem((512, FFP), bf16), vmem((4, 4, 32, 2304), bf16),
         mine] + reduce_scratch(4),
    )
    hidden_t, next_query, next_kv, kv_pages = local_call(
        next_layer, (fr, next_gain, next_query_weight, next_kv_weight, cosine, sine, page), [VM] * 7,
        [(288, 256), (256, 256), (256, 256), (2, 128, 256)],
    )
    return (hidden_t.T, next_query, next_kv, kv_pages)


def solution(mesh):
    wide = P("seq", "tensor")
    cols = P(None, "tensor")
    in_specs = (wide, P(), cols, cols, P("tensor", None), P(), P(), P(), wide, wide, wide, P(), cols, cols, P(), P(), P())
    out_specs = (wide, wide, wide, P("seq", None, "tensor"))
    return jax.shard_map(body, mesh=mesh, in_specs=in_specs, out_specs=out_specs, check_vma=False)
```

```python
import jax
import jax.numpy as jnp
from jax import lax
from jax.experimental import pallas as pl
from jax.experimental.pallas import tpu as pltpu
import numpy as np
from jax.sharding import PartitionSpec as P

EPS = 1e-06
SOFT_CAP = 50.0
MESH = pl.DeviceIdType.MESH
VM = pl.BlockSpec(memory_space=pltpu.VMEM)
AN = pl.BlockSpec(memory_space=pl.ANY)
FFP = 640
FFO = 512
bf16 = jnp.bfloat16
f32 = jnp.float32


class Place:
    def __init__(self):
        self.s = lax.axis_index("seq")
        self.t = lax.axis_index("tensor")
        self.x = self.s // 16
        self.z = (self.s // 2) % 8
        self.c = self.s % 2
        self.yb = self.t % 2
        self.X = self.x * 2 + self.t // 4
        self.Y = self.t % 4

    def grid(self, X, Y):
        return self.dev(self.seq(X // 2, self.z, self.c), (X % 2) * 4 + Y)

    def near(self, dim, sign, nx):
        if dim == 1:
            return self.grid(self.X, (self.Y + 4 + sign) % 4)
        if nx == 2:
            return self.dev(self.s, (self.t + 4) % 8)
        return self.grid((self.X + 4 + sign) % 4, self.Y)

    def around(self, nx):
        out = [self.near(1, 1, nx), self.near(1, -1, nx), self.near(0, 1, nx)]
        return out + ([self.near(0, -1, nx)] if nx == 4 else [])

    def seq(self, x, z, c):
        return x * 16 + z * 2 + c

    def dev(self, s, t):
        return {"seq": s, "tensor": t}

    def zp(self):
        return self.dev(self.seq(self.x, (self.z + 1) % 8, self.c), self.t)

    def zm(self):
        return self.dev(self.seq(self.x, (self.z + 7) % 8, self.c), self.t)

    def sib(self):
        return self.dev(self.seq(self.x, self.z, 1 - self.c), self.t)

    def xpart(self):
        return self.dev(self.seq(1 - self.x, self.z, self.c), self.t)

    def quad(self, o):
        dx, dy = o // 2, o % 2
        x = (self.x + dx) % 2
        yb = (self.yb + dy) % 2
        return x, yb, self.dev(self.seq(x, self.z, self.c), self.t - self.yb + yb)

    def tens(self, o):
        t = (self.t + o) % 8
        return t, self.dev(self.s, t)

    def plane(self, o):
        j = (self.x * 8 + self.t + o) % 16
        x, t = j // 8, j % 8
        return j, self.dev(self.seq(x, self.z, self.c), t)


class Copies:
    def __init__(self, send, recv):
        self.send, self.recv, self.n, self.live = send, recv, 0, []

    def make(self, src, dst, dev):
        i = self.n
        self.n += 1
        assert i < self.send.shape[0]
        return pltpu.make_async_remote_copy(
            src_ref=src, dst_ref=dst, send_sem=self.send.at[i], recv_sem=self.recv.at[i],
            device_id=dev, device_id_type=MESH,
        )

    def go(self, src, dst, dev):
        cp = self.make(src, dst, dev)
        cp.start()
        self.live.append(cp)
        return cp

    def drain_sends(self):
        for cp in self.live:
            cp.wait_send()


def barrier(peers):
    sem = pltpu.get_barrier_semaphore()
    for dev in peers:
        pl.semaphore_signal(sem, inc=1, device_id=dev, device_id_type=MESH)
    pl.semaphore_wait(sem, len(peers))


def gather_grid(p, cps, own, view, nx, middle=lambda: None):
    size = (nx, 4)

    def send(h, a, b, sub, dim, sign):
        dx, dy = (a, b) if h == 0 else (b, a)
        dst = view(dx, dy, h, sub)
        return cps.go(own(h) if (a, b) == (0, 0) else dst, dst, p.near(dim, sign, nx))

    def spread(h, a, b, dim):
        return [send(h, a, b, None, dim, sign) for sign in ((1, -1) if size[dim] == 4 else (1,))]

    first = [spread(h, 0, 0, h) for h in range(2)]
    second = [{0: spread(h, 0, 0, 1 - h)} for h in range(2)]
    far = [[], []]
    last = []
    for i in range(2):
        for h in range(2):
            if i < len(first[h]):
                first[h][i].wait_recv()
                a = (-1, 1)[i]
                if size[h] == 4:
                    far[h].append(send(h, a, 0, i, h, -a))
                second[h][a] = spread(h, a, 0, 1 - h)

    def onward(h, a):
        for i, cp in enumerate(second[h][a]):
            cp.wait_recv()
            if size[1 - h] == 4:
                b = (-1, 1)[i]
                last.append(send(h, a, b, i, 1 - h, -b))

    for h in range(2):
        onward(h, 0)
    middle()
    for h in range(2):
        if far[h]:
            for cp in far[h]:
                cp.wait_recv()
            second[h][2] = spread(h, 2, 0, 1 - h)
    for a in (-1, 1, 2):
        for h in range(2):
            if a in second[h]:
                onward(h, a)
    for cp in last:
        cp.wait_recv()


ROW = (slice(0, 16), slice(16, 32))
COL = (slice(0, 1152), slice(1152, 2304))


def reduce_line(p, cps, read, view, buf, dim, nx):
    size = (nx, 4)[dim]
    rp, rm, up, dn, bu, bd = buf
    plus, minus = p.near(dim, 1, nx), p.near(dim, -1, nx)
    if size == 2:
        cp = cps.go(view(1, None), rp, plus)

        def finish():
            cp.wait_recv()
            return read(0, None) + rp[...].astype(f32)

        return [finish]
    far0 = cps.go(view(2, 0), up, plus)
    far1 = cps.go(view(2, 1), dn, minus)
    near = [cps.go(view(1, 1), rp.at[:, ROW[1]], plus), cps.go(view(-1, 0), rm.at[:, ROW[0]], minus)]

    def relay():
        far0.wait_recv()
        bu[...] = (read(1, 0) + up[...].astype(f32)).astype(bf16)
        near.append(cps.go(bu, rp.at[:, ROW[0]], plus))
        far1.wait_recv()
        bd[...] = (read(-1, 1) + dn[...].astype(f32)).astype(bf16)
        near.append(cps.go(bd, rm.at[:, ROW[1]], minus))

    def finish():
        for cp in near:
            cp.wait_recv()
        return read(0, None) + rp[...].astype(f32) + rm[...].astype(f32)

    return [relay, finish]


def reduce_grid(p, cps, part, bufs, sums, nx):
    at = (p.X if nx == 4 else p.X % 2, p.Y)
    size = (nx, 4)

    def one(h):
        def view(d, sub):
            rows = slice(0, 32) if sub is None else ROW[sub]
            i = (at[1 - h] + size[1 - h] + d) % size[1 - h]
            return part.at[:, i, rows, COL[h]] if h == 0 else part.at[i, :, rows, COL[h]]

        def read(d, sub):
            return view(d, sub)[...].astype(f32)

        return reduce_line(p, cps, read, view, bufs[h][:6], 1 - h, nx)

    def two(h):
        def view(d, sub):
            rows = slice(0, 32) if sub is None else ROW[sub]
            i = (at[h] + size[h] + d) % size[h]
            return sums[h].at[pl.ds(i, 1), rows]

        def read(d, sub):
            return view(d, sub)[...].astype(f32)

        return reduce_line(p, cps, read, view, bufs[h][6:], h, nx)

    steps = [one(h) for h in range(2)]
    for h in range(2):
        if len(steps[h]) == 2:
            steps[h][0]()
    later = []
    for h in range(2):
        sums[h][...] = steps[h][-1]().astype(bf16)
        later.append(two(h))
    for h in range(2):
        if len(later[h]) == 2:
            later[h][0]()
    return [later[h][-1]()[0] for h in range(2)]


def reduce_scratch(nx):
    out = []
    for h in range(2):
        size = (nx, 4)
        for n, m in ((size[h], size[1 - h]), (1, size[h])):
            del m
            out += [pltpu.VMEM((n, 32, 1152), bf16)] * 2 + [pltpu.VMEM((n, 16, 1152), bf16)] * 4
        out.append(pltpu.VMEM((size[h], 32, 1152), bf16))
    return out


def reduce_bufs(refs):
    return [refs[0:12], refs[13:25]], [refs[12], refs[25]]


def normed(values, gain):
    return values * lax.rsqrt(jnp.mean(values * values, axis=1, keepdims=True) + EPS) * gain[...][None, :]


def strip(org, slot):
    return pl.ds(pl.multiple_of((org * 16 + slot) * 72, 8), 72)


def weight_send(p, cps, ws, own, d):
    org = p.x if own else 1 - p.x
    got = []
    for sign, dev in ((-1, p.zp()), (1, p.zm())):
        if d == 4 and (sign == -1) != own:
            continue
        here = strip(org, ((p.z + 8 + sign * (d - 1)) % 8) * 2 + p.c)
        got += [(cps.go(w.at[here], w.at[here], dev), w, sign) for w in ws]
    return org, got, d


def weight_take(p, cps, sent):
    org, got, d = sent
    out = []
    for cp, w, sign in got:
        cp.wait_recv()
        here = w.at[strip(org, ((p.z + 8 + sign * d) % 8) * 2 + p.c)]
        out.append(cps.go(here, here, p.sib()))
    return out


FREQ = (10000.0 ** (-np.arange(128, dtype=np.float64) / 128)).astype(np.float32)[None, :]


def starts_of(tags, e0, e1, e2):
    return jnp.where(tags >= e2, e2, jnp.where(tags >= e1, e1, jnp.where(tags >= e0, e0, 0)))


def whole_layer(
    lengths, owner, table, ht, gate, up, down, freq, attn_gain, wq, wk, wo, post_gain, ff_gain, last_gain,
    fr, wg, wu, wd, page_out, cosine, sine,
    send, recv, loc, xt, rows_ref, stay, go, q_ref, kv, qa, start_ref, acc, den, num, dn, pg, rn, rd, rp, part, mine,
    mid, xa, vg, vu, vd, inner, y_ref, final, *scratch,
):
    p = Place()
    quads = [p.quad(o) for o in range(1, 4)]
    barrier(p.around(4) + [d for _, _, d in quads[1:]] + [p.zp(), p.zm(), p.sib()])
    cps = Copies(send, recv)
    ws = (wg, wu, wd)
    slot = p.z * 2 + p.c
    near_rows = strip(p.x, slot)
    far_rows = strip(1 - p.x, slot)

    columns = pl.ds(pl.multiple_of(p.x * FFO, 128), FFP)
    other = pl.ds(pl.multiple_of((1 - p.x) * FFO, 128), FFP)
    swaps = [cps.go(a.at[:, other], w.at[near_rows], p.xpart()) for a, w in zip((gate, up, down), ws)]
    ring = [(cps.go(a.at[:, columns], w.at[near_rows], dev), w, sign)
            for sign, dev in ((-1, p.zp()), (1, p.zm())) for a, w in zip((gate, up, down), ws)]
    locs = [pltpu.make_async_copy(a.at[:, columns], w.at[near_rows], loc.at[i])
            for i, (a, w) in enumerate(zip((gate, up, down), ws))]
    locs.append(pltpu.make_async_copy(ht, xt.at[p.t], loc.at[3]))
    sib = [cps.go(a.at[:, columns], w.at[near_rows], p.sib()) for a, w in zip((gate, up, down), ws)]
    for cp in locs:
        cp.start()

    e0 = lengths[0]
    e1 = e0 + lengths[1]
    e2 = e1 + lengths[2]
    row = lax.broadcasted_iota(jnp.int32, (128, 128), 0)
    lane = lax.broadcasted_iota(jnp.int32, (128, 128), 1)
    mypair = owner[p.s]
    for blk in range(2):
        tag = (mypair if blk == 0 else 63 - mypair) * 128 + row
        angle = (tag - starts_of(tag, e0, e1, e2)).astype(f32) * freq[...]
        cosine[blk * 128:(blk + 1) * 128, :] = jnp.cos(angle)
        sine[blk * 128:(blk + 1) * 128, :] = jnp.sin(angle)
    q_blocks = []
    for x in range(2):
        b = owner[x * 16 + p.z * 2 + p.c]
        q_blocks += [b, 63 - b]
    for n in range(4):
        start = starts_of(q_blocks[n] * 128 + row, e0, e1, e2)
        start_ref[n, 0:128, :] = start
        start_ref[n, 128:256, :] = start

    def view_hidden(dx, dy, h, sub):
        t = ((p.t // 4 + 2 + dx) % 2) * 4 + (p.Y + 4 + dy) % 4
        low, n = ((0, 144) if sub is None else ((0, 80), (80, 64))[sub])
        return xt.at[t, pl.ds(h * 144 + low, n)]

    swapped = []

    def middle():
        for cp in swaps:
            cp.wait_recv()
        swapped.append(weight_send(p, cps, ws, False, 1))
        for w in ws:
            sib.append(cps.go(w.at[far_rows], w.at[far_rows], p.sib()))

    gather_grid(p, cps, lambda h: ht.at[pl.ds(h * 144, 144)], view_hidden, 2, middle)
    locs[3].wait()

    rows = jnp.transpose(xt[...].reshape(2304, 256).astype(f32))
    rows_ref[...] = rows.astype(bf16).reshape(8, 32, 2304)
    normal = normed(rows, attn_gain).astype(bf16)
    own = turned(jnp.dot(normal, wk[...], preferred_element_type=f32), cosine, sine, p.yb == 0)
    low = (p.yb + p.z) % 2 == 0
    stay[...] = jnp.where(low, own[:128], own[128:]).astype(bf16)
    go[...] = jnp.where(low, own[128:], own[:128]).astype(bf16)
    ends = ((7, p.zp()), (1, p.zm()), (0, p.sib()))
    pair = cps.go(go, kv.at[p.yb, 0, p.c], quads[0][2])
    first = [cps.go(stay, kv.at[p.yb, r, p.c], dev) for r, dev in ends]
    got, shared = [first[:2]], [first[2:]]
    lq = [pltpu.make_async_copy(stay, kv.at[p.yb, 0, p.c], loc.at[4])]
    lq[0].start()
    query = turned(jnp.dot(normal, wq[...], preferred_element_type=f32), cosine, sine, None)
    q_ref[...] = query.astype(bf16).reshape(2, 128, 256)
    lq.append(pltpu.make_async_copy(q_ref, qa.at[p.x, p.yb], loc.at[5]))
    lq[1].start()
    pair.wait_recv()
    mate = kv.at[1 - p.yb, 0, p.c]
    first = [cps.go(mate, kv.at[1 - p.yb, r, p.c], dev) for r, dev in ends]
    got.append(first[:2])
    shared[0] += first[2:]
    qs = [cps.go(q_ref, qa.at[p.x, p.yb], d) for _, _, d in quads]
    acc[...] = jnp.zeros_like(acc)
    den[...] = jnp.zeros_like(den)
    for cp in lq:
        cp.wait()
    for cp in qs:
        cp.wait_recv()

    def key_block(z, c):
        b = owner[p.x * 16 + z * 2 + c]
        return jnp.where((p.yb + z) % 2 == 0, b, 63 - b)

    def attend(rel):
        z = (p.z + rel) % 8
        blocks = [key_block(z, c) for c in range(2)]
        keys = kv[0, rel].reshape(256, 256)
        values = kv[1, rel].reshape(256, 256)

        def tile(n, carry):
            b = owner[(n // 2) * 16 + p.z * 2 + p.c]
            q_block = jnp.where(n % 2 == 0, b, 63 - b)
            qt = jnp.concatenate([qa[n // 2, h, n % 2] for h in range(2)], axis=0)
            score = lax.dot_general(qt, keys, (((1,), (1,)), ((), ())), preferred_element_type=f32)
            weight = jnp.exp(SOFT_CAP * jnp.tanh(score * (0.0625 / SOFT_CAP)))
            start = start_ref[n]
            r = lax.broadcasted_iota(jnp.int32, (256, 128), 0) % 128
            l = lax.broadcasted_iota(jnp.int32, (256, 128), 1)
            rounded = []
            for c in range(2):
                kt = blocks[c] * 128 + l
                ok = (kt <= q_block * 128 + r) & (kt >= start)
                rounded.append(jnp.where(ok, weight[:, c * 128:(c + 1) * 128], 0.0).astype(bf16))
            den[n] += rounded[0].astype(f32) + rounded[1].astype(f32)
            acc[n] += jnp.dot(jnp.concatenate(rounded, axis=1), values, preferred_element_type=f32)
            return carry

        lax.fori_loop(0, 4, tile, 0)

    spots = [[0]]
    for d in range(1, 5):
        nxt = [[], []]
        now = []
        for i, kind in enumerate((p.yb, 1 - p.yb)):
            for side, cp in enumerate(got[i]):
                cp.wait_recv()
                rel = 8 - d if side == 0 else d
                here = kv.at[kind, rel, p.c]
                if d < 3 or (d == 3 and side == i):
                    further = kv.at[kind, rel - 1 if side == 0 else rel + 1, p.c]
                    nxt[i].append(cps.go(here, further, (p.zp(), p.zm())[side]))
                now.append(cps.go(here, here, p.sib()))
        got = nxt
        if d == 4:
            sib += weight_take(p, cps, (p.x, ring, 1))
            sib += weight_take(p, cps, swapped[0])
            rest = [weight_send(p, cps, ws, True, 2), weight_send(p, cps, ws, False, 2)]
        for cp in shared[d - 1]:
            cp.wait_recv()
        for rel in spots[d - 1]:
            attend(rel)
        shared.append(now)
        spots.append([8 - d, d] if d < 4 else [4])
    for cp in shared[4]:
        cp.wait_recv()
    attend(4)

    for n in range(4):
        below = lax.dot_general(
            jnp.ones((8, 128), f32), den[n], (((1,), (1,)), ((), ())),
            precision=lax.Precision.HIGHEST, preferred_element_type=f32,
        )
        for h in range(2):
            num[n // 2, h, n % 2] = acc[n, h * 128:(h + 1) * 128, :].astype(bf16)
            dn[n // 2, h, n % 2] = below[:, h * 128:(h + 1) * 128]
    ex = [cps.go(num.at[x, yb], rn.at[o], d) for o, (x, yb, d) in enumerate(quads)]
    ex += [cps.go(dn.at[x, yb], rd.at[o], d) for o, (x, yb, d) in enumerate(quads)]
    base = p.z * 4 + p.c * 2

    def look(i, found):
        page = table[i]
        return tuple(jnp.where(page == (n // 2) * 32 + base + n % 2, i, f) for n, f in enumerate(found))

    wanted = lax.fori_loop(0, 64, look, (jnp.int32(0),) * 4)

    def choose(n, carry):
        want = jnp.where(n == 0, wanted[0], jnp.where(n == 1, wanted[1], jnp.where(n == 2, wanted[2], wanted[3])))
        sums = [jnp.zeros((128, 256), f32)] * 2
        for rel in range(8):
            for c in range(2):
                take = jnp.where(key_block((p.z + rel) % 8, c) == want, 1.0, 0.0)
                sums = [a + kv[kind, rel, c].astype(f32) * take for kind, a in enumerate(sums)]
        for kind in range(2):
            pg[n // 2, kind, n % 2] = sums[kind].astype(bf16)
        return carry

    lax.fori_loop(0, 4, choose, 0)
    for cp in ex:
        cp.wait_recv()
    total = num[p.x, p.yb].astype(f32)
    below = dn[p.x, p.yb]
    for o in range(3):
        total += rn[o].astype(f32)
        below += rd[o]
    pieces = []
    for blk in range(2):
        inverse = jnp.transpose(jnp.broadcast_to(1.0 / below[blk, 0:1, :], (128, 128)))
        pieces.append((total[blk] * jnp.concatenate([inverse, inverse], axis=1)).astype(bf16))
    attended = jnp.concatenate(pieces, axis=0)
    part[...] = jnp.dot(attended, wo[...], preferred_element_type=f32).astype(bf16).reshape(2, 4, 32, 2304)
    sib += weight_take(p, cps, rest[0])
    sib += weight_take(p, cps, rest[1])
    rest = [weight_send(p, cps, ws, True, 3), weight_send(p, cps, ws, False, 3)]

    bufs, sums = reduce_bufs(scratch[:26])
    total = jnp.concatenate(reduce_grid(p, cps, part, bufs, sums, 2), axis=1)
    middle_rows = (rows_ref[p.t].astype(f32) + normed(total, post_gain)).astype(bf16)
    mid[...] = middle_rows
    mine[...] = normed(middle_rows.astype(f32), ff_gain).astype(bf16)
    lc = pltpu.make_async_copy(mine, xa.at[p.X, p.Y], loc.at[6])
    lc.start()
    last = []

    def view(dx, dy, h, sub):
        rows = slice(0, 32) if sub is None else ROW[sub]
        return xa.at[(p.X + 4 + dx) % 4, (p.Y + 4 + dy) % 4, rows, COL[h]]

    def middle_step():
        sib.extend(weight_take(p, cps, rest[0]))
        last.append(weight_send(p, cps, ws, True, 4))
        sib.extend(weight_take(p, cps, rest[1]))
        last.append(weight_send(p, cps, ws, False, 4))

    gather_grid(p, cps, lambda h: mine.at[:, COL[h]], view, 4, middle_step)
    sib += weight_take(p, cps, last[0])
    sib += weight_take(p, cps, last[1])
    for cp in sib:
        cp.wait_recv()
    for cp in locs[:3] + [lc]:
        cp.wait()
    loads = [pltpu.make_async_copy(w, v, loc.at[7 + i]) for i, (w, v) in enumerate(((wg, vg), (wu, vu), (wd, vd)))]
    for cp in loads:
        cp.start()
    px = [cps.go(pg.at[x, yb], rp.at[o], d) for o, (x, yb, d) in enumerate(quads)]
    loads[0].wait()
    loads[1].wait()

    def block(j, carry):
        cols = pl.ds(pl.multiple_of(j * 128, 128), 128)
        pair_cols = jnp.concatenate([vg[:, cols], vu[:, cols]], axis=1)
        both = jnp.dot(xa[...].reshape(512, 2304), pair_cols, preferred_element_type=f32)
        made = jax.nn.gelu(both[:, :128], approximate=True) * both[:, 128:]
        keep = jnp.zeros(made.shape, jnp.int32) + (j + 1 - p.x) > 0
        inner[:, cols] = jnp.where(keep, made, 0.0).astype(bf16)
        return carry

    lax.fori_loop(0, 5, block, 0)
    loads[2].wait()

    def lower(n, carry):
        w = vd[pl.ds(pl.multiple_of(n * 256, 256), 256), :]
        out = lax.dot_general(inner[...], w, (((1,), (1,)), ((), ())), preferred_element_type=f32)
        y_ref[:, :, :, pl.ds(pl.multiple_of(n * 256, 256), 256)] = out.astype(bf16).reshape(4, 4, 32, 256)
        return carry

    lax.fori_loop(0, 9, lower, 0)
    bufs, sums = reduce_bufs(scratch[26:])
    total = jnp.concatenate(reduce_grid(p, cps, y_ref, bufs, sums, 4), axis=1)
    final[...] = (mid[...].astype(f32) + normed(total, last_gain)).astype(bf16)
    lc = pltpu.make_async_copy(final, fr.at[p.t], loc.at[10])
    lc.start()

    def view_final(dx, dy, h, sub):
        rows = slice(0, 32) if sub is None else ROW[sub]
        return fr.at[((p.X + 2 + dx) % 2) * 4 + (p.Y + 4 + dy) % 4, rows, COL[h]]

    gather_grid(p, cps, lambda h: final.at[:, COL[h]], view_final, 2)
    for cp in px:
        cp.wait_recv()
    pages = pg[p.x, p.yb].astype(f32)
    for o in range(3):
        pages += rp[o].astype(f32)
    page_out[...] = pages.astype(bf16)
    lc.wait()
    cps.drain_sends()


def turned(v, cosine, sine, turn):
    c, s = cosine[...], sine[...]
    if turn is not None:
        c = jnp.where(turn, c, 1.0)
        s = jnp.where(turn, s, 0.0)
    a, b = v[:, :128], v[:, 128:]
    return jnp.concatenate([a * c - b * s, b * c + a * s], axis=1)


def call(body, cid, ins, in_specs, outs, out_specs, n, n_loc=0, aliases=None, extra=()):
    scratch = [pltpu.SemaphoreType.DMA((n,)), pltpu.SemaphoreType.DMA((n,))]
    if n_loc:
        scratch.append(pltpu.SemaphoreType.DMA((n_loc,)))
    return pl.pallas_call(
        body,
        out_shape=[s if isinstance(s, jax.ShapeDtypeStruct) else jax.ShapeDtypeStruct(s, bf16) for s in outs],
        in_specs=in_specs,
        out_specs=out_specs,
        scratch_shapes=scratch + list(extra),
        input_output_aliases=aliases or {},
        compiler_params=pltpu.CompilerParams(collective_id=cid, has_side_effects=True),
        name=body.__name__,
    )(*ins)


def next_layer(fr, gain, wq, wk, cosine, sine, page, ho, q_ref, k_ref, page_out):
    p = Place()
    rows = fr[...].reshape(256, 2304).astype(f32)
    normal = normed(rows, gain).astype(bf16)
    q_ref[...] = turned(jnp.dot(normal, wq[...], preferred_element_type=f32), cosine, sine, None).astype(bf16)
    k_ref[...] = turned(jnp.dot(normal, wk[...], preferred_element_type=f32), cosine, sine, p.yb == 0).astype(bf16)
    begin = p.t * 288
    tile = pl.multiple_of((begin // 128) * 128, 128)
    window = fr[:, :, pl.ds(tile, 384)].reshape(256, 384).astype(f32)
    moved = jnp.transpose(pltpu.roll(window, (384 - begin % 128) % 384, 1))
    ho[...] = moved[:288, :].astype(bf16)
    page_out[...] = page[...]


def local_call(body, ins, in_specs, outs, scratch=()):
    return pl.pallas_call(
        body,
        out_shape=[jax.ShapeDtypeStruct(s, bf16) for s in outs],
        in_specs=in_specs,
        out_specs=[VM] * len(outs),
        scratch_shapes=list(scratch),
        name=body.__name__,
    )(*ins)


def quad_route(dx, dy):
    route = []
    for s in range(32):
        for t in range(8):
            route.append((s * 8 + t, ((s + 16 * dx) % 32) * 8 + (t ^ dy)))
    return route


def body(
    hidden, attn_gain, query_weight, kv_weight, out_weight, post_gain, ff_gain, ff_post_gain,
    gate_weight, up_weight, down_weight_t, next_gain, next_query_weight, next_kv_weight,
    lengths, pair_owner, page_table,
):
    wshape = (2304, FFP)
    vmem = pltpu.VMEM
    angle = jax.ShapeDtypeStruct((256, 128), f32)
    mine = vmem((32, 2304), bf16)
    fr, wg, wu, wd, page, cosine, sine = call(
        whole_layer, 1,
        (lengths, pair_owner, page_table, hidden.T, gate_weight, up_weight, down_weight_t, jnp.asarray(FREQ), attn_gain,
         query_weight, kv_weight, out_weight, post_gain, ff_gain, ff_post_gain),
        [pl.BlockSpec(memory_space=pltpu.SMEM)] * 3 + [VM] * 12,
        [(8, 32, 2304), wshape, wshape, wshape, (2, 128, 256), angle, angle],
        [VM, AN, AN, AN, VM, VM, VM], 280, 11, None,
        [vmem((8, 288, 256), bf16), vmem((8, 32, 2304), bf16), vmem((128, 256), bf16), vmem((128, 256), bf16),
         vmem((2, 128, 256), bf16), vmem((2, 8, 2, 128, 256), bf16), vmem((2, 2, 2, 128, 256), bf16),
         vmem((4, 256, 128), jnp.int32), vmem((4, 256, 256), f32), vmem((4, 256, 128), f32),
         vmem((2, 2, 2, 128, 256), bf16), vmem((2, 2, 2, 8, 128), f32), vmem((2, 2, 2, 128, 256), bf16),
         vmem((3, 2, 128, 256), bf16), vmem((3, 2, 8, 128), f32), vmem((3, 2, 128, 256), bf16),
         vmem((2, 4, 32, 2304), bf16), mine, mine, vmem((4, 4, 32, 2304), bf16), vmem((2304, FFP), bf16),
         vmem((2304, FFP), bf16), vmem((2304, FFP), bf16), vmem((512, FFP), bf16), vmem((4, 4, 32, 2304), bf16), mine]
        + reduce_scratch(2) + reduce_scratch(4),
    )
    hidden_t, next_query, next_kv, kv_pages = local_call(
        next_layer, (fr, next_gain, next_query_weight, next_kv_weight, cosine, sine, page), [VM] * 7,
        [(288, 256), (256, 256), (256, 256), (2, 128, 256)],
    )
    return (hidden_t.T, next_query, next_kv, kv_pages)


def solution(mesh):
    wide = P("seq", "tensor")
    cols = P(None, "tensor")
    in_specs = (wide, P(), cols, cols, P("tensor", None), P(), P(), P(), wide, wide, wide, P(), cols, cols, P(), P(), P())
    out_specs = (wide, wide, wide, P("seq", None, "tensor"))
    return jax.shard_map(body, mesh=mesh, in_specs=in_specs, out_specs=out_specs, check_vma=False)
```
